256 devices in a mesh: row: 16 (over y_lo, z), col: 16 (over y_hi, x, core).
Axes of the slice: x: 4, y: 4 (y_hi: 2, y_lo: 2; y = y_hi * 2 + y_lo), z: 8, core: 2. Of those that a mesh axis runs over, the one named last changes fastest.
Arguments:
- spectra: bfloat16 [2, 2, 10240, 256], P(None, None, ('row', 'col')), may hold values from -40 to 40
- delays_s: int32 [10240, 512], P('row'), may hold values from 0 to 1023
- delays_r: int32 [10240, 512], P('col'), may hold values from 0 to 1023
- wl_index: int32 [2], replicated, may hold values from 0 to 10239
Outputs:
- beam_field: float32 [2, 2, 512, 512], P(None, None, 'col', 'row')
The draws below stay inside these ranges and needn't reach their ends.
All inputs are finite; a program needn't handle non-finite values.
Results may differ from the reference program's by a relative error of at most 0.0071.
Values may be sent and summed in bfloat16 or wider, within the bound.
A program may use at most 64 MiB of HBM per device.

```python
import math
import jax
import jax.numpy as jnp
from jax import lax

FREQS = 2
STATIONS = 10240
WINDOWS = 256
BEAMS_R = 512
BEAMS_S = 512
N_ROW = 16
N_COL = 16


def draw_spectra(key, part):
    first, second = jax.random.split(key, 2)
    scales = jnp.exp(jax.random.uniform(second, (FREQS, 1, STATIONS, 1), jnp.float32, 0.0, math.log(10.0)))
    values = scales * jax.random.normal(first, (FREQS, 2, STATIONS, WINDOWS), jnp.float32)
    return jnp.clip(values, -40.0, 40.0).astype(jnp.bfloat16)


def touch_ends(entries, rng, smallest, largest):
    longest = entries.shape.index(max(entries.shape))
    spots = []
    for shift in (0, 1):
        where = [jax.random.randint(jax.random.fold_in(rng, axis), (), 0, length) for axis, length in enumerate(entries.shape)]
        where[longest] = (where[longest] + shift) % entries.shape[longest]
        spots.append(tuple(where))
    return entries.at[spots[0]].set(smallest).at[spots[1]].set(largest)


def setup_inputs(seed: int = 0) -> dict:
    key_of = jax.random.split(jax.random.key(seed), 5)
    spectra = draw_spectra(jax.random.fold_in(key_of[4], 71), 0)
    delays_s = touch_ends(jax.random.randint(key_of[1], (STATIONS, BEAMS_S), 0, 1024), jax.random.fold_in(key_of[1], 1), 0, 1023).astype(jnp.int32)
    delays_r = touch_ends(jax.random.randint(key_of[2], (STATIONS, BEAMS_R), 0, 1024), jax.random.fold_in(key_of[2], 1), 0, 1023).astype(jnp.int32)
    wl_index = jax.random.randint(key_of[3], (FREQS,), 0, STATIONS).astype(jnp.int32)
    return {"spectra": spectra, "delays_s": delays_s, "delays_r": delays_r, "wl_index": wl_index}


cycle_rates = (0.0361, 0.0596)
two_pi = 2.0 * math.pi

def steering(delays):
    rates = jnp.array(cycle_rates, jnp.float32)
    phase = (two_pi * rates)[:, None, None] * delays.astype(jnp.float32)[None]
    return (jnp.cos(phase).astype(jnp.bfloat16), jnp.sin(phase).astype(jnp.bfloat16))

def product(form, left, right):
    return jnp.einsum(form, left.astype(jnp.float32), right.astype(jnp.float32), precision=lax.Precision.HIGHEST)

def reference(spectra, delays_s, delays_r, wl_index):
    values = spectra.astype(jnp.float32)
    power = lax.optimization_barrier(jnp.sum(jnp.square(values), axis=(1, 3)))
    level = 0.5 * power[jnp.arange(FREQS, dtype=jnp.int32), wl_index]
    gain = lax.rsqrt(power + level[:, None])
    per_station = STATIONS // (N_ROW * N_COL)
    natural_r = delays_r.reshape(N_COL, N_ROW, per_station, BEAMS_R).transpose(1, 0, 2, 3).reshape(STATIONS, BEAMS_R)
    rec_cos, rec_sin = steering(natural_r)
    src_cos, src_sin = steering(delays_s)
    rec_cos = rec_cos.astype(jnp.float32)
    rec_sin = rec_sin.astype(jnp.float32)
    block = STATIONS // N_ROW

    def one_block(total, index):
        start = (index * block).astype(jnp.int32)
        rows = lax.dynamic_slice_in_dim(values, start, block, 2)
        row_gain = lax.dynamic_slice_in_dim(gain, start, block, 1)
        cross_re = product('fiw,fjw->fij', rows[:, 0], values[:, 0]) + product('fiw,fjw->fij', rows[:, 1], values[:, 1])
        cross_im = product('fiw,fjw->fij', rows[:, 1], values[:, 0]) - product('fiw,fjw->fij', rows[:, 0], values[:, 1])
        weight = row_gain[:, :, None] * gain[:, None, :]
        coh_re = lax.optimization_barrier((cross_re * weight).astype(jnp.bfloat16)).astype(jnp.float32)
        coh_im = lax.optimization_barrier((cross_im * weight).astype(jnp.bfloat16)).astype(jnp.float32)
        beam_re = product('fij,fjb->fib', coh_re, rec_cos) + product('fij,fjb->fib', coh_im, rec_sin)
        beam_im = product('fij,fjb->fib', coh_im, rec_cos) - product('fij,fjb->fib', coh_re, rec_sin)
        scos = lax.dynamic_slice_in_dim(src_cos, start, block, 1)
        ssin = lax.dynamic_slice_in_dim(src_sin, start, block, 1)
        out_re = product('fib,fia->fba', beam_re, scos) - product('fib,fia->fba', beam_im, ssin)
        out_im = product('fib,fia->fba', beam_im, scos) + product('fib,fia->fba', beam_re, ssin)
        return (total + jnp.stack([out_re, out_im], axis=1), None)
    empty = jnp.zeros((FREQS, 2, BEAMS_R, BEAMS_S), jnp.float32)
    total, _ = lax.scan(one_block, empty, jnp.arange(N_ROW, dtype=jnp.int32))
    return total * (math.sqrt(WINDOWS) / STATIONS)
```

```python
import functools
import math

import jax
import jax.numpy as jnp
from jax import lax
from jax.experimental import pallas as pl
from jax.experimental.pallas import tpu as pltpu
from jax.sharding import PartitionSpec as P

MESH = pl.DeviceIdType.MESH
F32 = jnp.float32
BF16 = jnp.bfloat16

STATIONS = 10240
WINDOWS = 256
SIDE = 16
OWN = 40
SLOT = 48
HALF = 256
BEAMS = 32
RATES = (0.0361, 0.0596)

COS = (0.9999992215668542, -19.7389825153523, 64.92872658489378, -85.27239662504564, 58.79403695210448, -21.076779298561963)
SIN = (6.283182818541802, -41.34142139793358, 81.59618385577838, -76.58010036540968, 41.20539421297601, -12.271261390344423)

PW_ROW, PW_COL, X_ROW, X_COL, LV_COL, SUM_U, SUM_V, ALL_U, ALL_V = range(9)


def horner(coefs, z):
    acc = jnp.full_like(z, coefs[-1])
    for c in coefs[-2::-1]:
        acc = acc * z + c
    return acc


def kernel(
    spec_hbm, ds_hbm, dr_hbm, wl, out,
    xin, dbuf, tab, pk, xr, pw_send, pw, lv_send, lv, sums, part, block, gathered,
    load, send, recv,
):
    r, c = lax.axis_index("row"), lax.axis_index("col")
    slots = (c // 2, r // 2)
    halves = (c % 2, r % 2)
    holder = (r // 8 == halves[0], c // 8 == halves[1])
    place = (c, r)
    rank = (r, c)

    def peer(axis, other):
        return (r, other) if axis == 0 else (other, c)

    def copy(src, dst, group, s, t, device):
        return pltpu.make_async_remote_copy(
            src_ref=src, dst_ref=dst, send_sem=send.at[group, s], recv_sem=recv.at[group, t],
            device_id=device, device_id_type=MESH,
        )

    def over_peers(axis, action):
        def step(o, carry):
            action(lax.rem(place[axis] + o, SIDE))
            return carry

        lax.fori_loop(1, SIDE, step, 0)

    def load_delays(hbm, which):
        start = pl.multiple_of(halves[which] * HALF, HALF)
        return pltpu.make_async_copy(hbm.at[:, pl.ds(start, HALF)], dbuf.at[which], load.at[which])

    loads = [load_delays(ds_hbm, 0), load_delays(dr_hbm, 1)]
    load_x = pltpu.make_async_copy(spec_hbm, xin, load.at[2])
    load_x.start()
    for item in loads:
        item.start()
    barrier = pltpu.get_barrier_semaphore()
    for axis in (0, 1):
        over_peers(axis, lambda p: pl.semaphore_signal(barrier, inc=1, device_id=peer(axis, p), device_id_type=MESH))

    load_x.wait()
    lane = lax.broadcasted_iota(jnp.int32, (OWN, 128), 1)
    low = lane < 64
    column = jnp.zeros((OWN, 128), F32)
    for f in range(2):
        tiles = [[xin[f, p, :, 128 * t : 128 * t + 128].astype(F32) for t in range(2)] for p in range(2)]
        total = sum(tiles[p][t] * tiles[p][t] for p in range(2) for t in range(2))
        column = jnp.where(lane == f, jnp.sum(total, axis=1, keepdims=True), column)
        for t in range(2):
            re, im = tiles[0][t], tiles[1][t]
            first = jnp.where(low, re, pltpu.roll(im, 64, 1))
            second = jnp.where(low, pltpu.roll(re, 64, 1), im)
            for k, value in ((2 * t, first), (2 * t + 1, second)):
                pk[4 * f + k] = jnp.concatenate([value, jnp.zeros((SLOT - OWN, 128), F32)], axis=0).astype(BF16)
    rows = jnp.concatenate([column, jnp.zeros((128 - OWN, 128), F32)], axis=0).T[:8]
    station = (r * SIDE + c) * OWN + lax.broadcasted_iota(jnp.int32, (8, 128), 1)
    sub = lax.broadcasted_iota(jnp.int32, (8, 128), 0)
    inside = lax.broadcasted_iota(jnp.int32, (8, 128), 1) < OWN
    wanted = jnp.where(sub == 0, wl[0], wl[1])
    picked = jnp.sum(jnp.where(inside & (station == wanted) & (sub < 2), rows, 0.0), axis=1, keepdims=True)
    tile = jnp.where(sub < 2, rows, pltpu.roll(jnp.broadcast_to(picked, (8, 128)), 2, 0))
    pw_send[...] = tile

    pl.semaphore_wait(barrier, 2 * (SIDE - 1))

    for axis, group in ((0, PW_ROW), (1, PW_COL)):
        over_peers(axis, lambda p: copy(pw_send, pw.at[axis, place[axis]], group, p, place[axis], peer(axis, p)).start())
        pw[axis, place[axis]] = tile
    for axis, group in ((0, X_ROW), (1, X_COL)):
        over_peers(axis, lambda p: copy(pk.at[p // 2], xr.at[axis, place[axis]], group, p, place[axis], peer(axis, p)).start())
        xr[axis, place[axis]] = pk[place[axis] // 2]

    def steer(which):
        loads[which].wait()
        rate = jnp.where(slots[which] // 4 == 0, RATES[0], RATES[1]).astype(F32)

        def step(q, carry):
            turns = dbuf[which, pl.ds(pl.multiple_of(q * OWN, 8), OWN), :].astype(F32) * rate
            x = turns - jnp.round(turns)
            z = x * x
            pad = jnp.zeros((SLOT - OWN, HALF), F32)
            at = pl.ds(pl.multiple_of(q * SLOT, SLOT), SLOT)
            tab[which, at, :HALF] = jnp.concatenate([horner(COS, z), pad], axis=0).astype(BF16)
            tab[which, at, HALF:] = jnp.concatenate([horner(SIN, z) * x, pad], axis=0).astype(BF16)
            return carry

        lax.fori_loop(0, SIDE, step, 0)

    steer(0)
    over_peers(0, lambda p: copy(pw_send, pw.at[0, p], PW_ROW, p, p, peer(0, p)).wait_recv())
    lv_tile = jnp.sum(pw[0], axis=0)
    lv_send[...] = lv_tile
    over_peers(1, lambda p: copy(lv_send, lv.at[r], LV_COL, p, r, peer(1, p)).start())
    lv[r] = lv_tile
    steer(1)
    over_peers(1, lambda p: copy(pw_send, pw.at[1, p], PW_COL, p, p, peer(1, p)).wait_recv())
    for axis, group in ((0, X_ROW), (1, X_COL)):
        over_peers(axis, lambda p: copy(pk.at[0], xr.at[axis, p], group, p, p, peer(axis, p)).wait_recv())
    over_peers(1, lambda p: copy(lv_send, lv.at[p], LV_COL, p, p, peer(1, p)).wait_recv())
    level = 0.5 * jnp.sum(lv[...], axis=0)

    for which, group in ((0, SUM_U), (1, SUM_V)):
        first = slots[which] // 4 == 0
        power = jnp.where(first, pw[which, :, 0, :], pw[which, :, 1, :])
        lev = jnp.where(first, level[2:3], level[3:4])
        used = lax.broadcasted_iota(jnp.int32, (SIDE, 128), 1) < OWN
        gain = jnp.where(used, lax.rsqrt(power + lev), 0.0)
        gain = jnp.concatenate([gain, jnp.zeros((128 - SIDE, 128), F32)], axis=0).T[:SLOT]
        scaled = jnp.concatenate(
            [(xr[which, q].astype(F32) * gain[:, q : q + 1]).astype(BF16) for q in range(SIDE)], axis=0
        )
        sums_t = lax.dot_general(
            scaled, tab[which], (((0,), (0,)), ((), ())), preferred_element_type=F32
        )
        re = sums_t[:64, :HALF] - sums_t[64:, HALF:]
        im = sums_t[64:, :HALF] + sums_t[:64, HALF:]
        value = jnp.concatenate([re, im], axis=0)
        for h in range(2):
            turned = value[:, 128 * h : 128 * h + 128].T.astype(BF16)
            for j in range(4):
                sums[which, 4 * h + j] = turned[BEAMS * j : BEAMS * j + BEAMS]
        other = 1 - which
        mine = place[other]

        def send_sum(j, carry):
            target = halves[which] * 8 + j

            @pl.when(target != mine)
            def _():
                copy(sums.at[which, j], part.at[which, mine], group, j, mine, peer(other, target)).start()

            return carry

        lax.fori_loop(0, 8, send_sum, 0)

        @pl.when(holder[which])
        def _():
            part[which, mine] = sums[which, lax.rem(mine, 8)]

    for which, group, after in ((0, SUM_U, ALL_U), (1, SUM_V, ALL_V)):
        other = 1 - which

        @pl.when(holder[which])
        def _():
            over_peers(other, lambda p: copy(sums.at[which, 0], part.at[which, p], group, 0, p, peer(other, p)).wait_recv())
            total = jnp.sum(part[which].astype(F32), axis=0).astype(BF16)
            block[which] = total
            over_peers(
                which,
                lambda p: copy(
                    block.at[which], gathered.at[which, slots[which]], after, p, slots[which], peer(which, p)
                ).start(),
            )
            gathered[which, slots[which]] = total

    for which, after in ((0, ALL_U), (1, ALL_V)):
        half_here = rank[which] // 8

        def arrive(s, carry):
            @pl.when(2 * s + half_here != place[which])
            def _():
                copy(block.at[which], gathered.at[which, s], after, 0, s, peer(which, 2 * s + half_here)).wait_recv()

            return carry

        lax.fori_loop(0, 8, arrive, 0)

    low = lax.broadcasted_iota(jnp.int32, (BEAMS, 128), 1) < 64
    for f in range(2):
        acc = jnp.zeros((BEAMS, 2 * BEAMS), F32)
        for k in range(4):
            u = gathered[0, 4 * f + k]
            turned = pltpu.roll(u.astype(F32), 64, 1)
            turned = jnp.where(low, turned, -turned).astype(BF16)
            acc += lax.dot_general(
                gathered[1, 4 * f + k], jnp.concatenate([u, turned], axis=0),
                (((1,), (1,)), ((), ())), preferred_element_type=F32,
            )
        acc = acc * (math.sqrt(WINDOWS) / STATIONS)
        out[f, 0] = acc[:, :BEAMS]
        out[f, 1] = acc[:, BEAMS:]

    for axis, a, b, d in ((0, PW_ROW, X_ROW, None), (1, PW_COL, X_COL, LV_COL)):
        over_peers(axis, lambda p: copy(pw_send, pw.at[axis, p], a, p, p, peer(axis, p)).wait_send())
        over_peers(axis, lambda p: copy(pk.at[0], xr.at[axis, p], b, p, p, peer(axis, p)).wait_send())
        if d is not None:
            over_peers(axis, lambda p: copy(lv_send, lv.at[p], d, p, p, peer(axis, p)).wait_send())
    for which, group, after in ((0, SUM_U, ALL_U), (1, SUM_V, ALL_V)):
        other = 1 - which

        def sent(j, carry):
            target = halves[which] * 8 + j

            @pl.when(target != place[other])
            def _():
                copy(sums.at[which, j], part.at[which, 0], group, j, 0, peer(other, target)).wait_send()

            return carry

        lax.fori_loop(0, 8, sent, 0)

        @pl.when(holder[which])
        def _():
            over_peers(which, lambda p: copy(block.at[which], gathered.at[which, 0], after, p, 0, peer(which, p)).wait_send())


def body(spectra, delays_s, delays_r, wl_index):
    return pl.pallas_call(
        kernel,
        out_shape=jax.ShapeDtypeStruct((2, 2, BEAMS, BEAMS), F32),
        in_specs=[pl.BlockSpec(memory_space=pl.ANY)] * 3 + [pl.BlockSpec(memory_space=pltpu.SMEM)],
        out_specs=pl.BlockSpec(memory_space=pltpu.VMEM),
        scratch_shapes=[
            pltpu.VMEM((2, 2, OWN, WINDOWS), BF16),
            pltpu.VMEM((2, SIDE * OWN, HALF), jnp.int32),
            pltpu.VMEM((2, SIDE * SLOT, 2 * HALF), BF16),
            pltpu.VMEM((8, SLOT, 128), BF16),
            pltpu.VMEM((2, SIDE, SLOT, 128), BF16),
            pltpu.VMEM((8, 128), F32),
            pltpu.VMEM((2, SIDE, 8, 128), F32),
            pltpu.VMEM((8, 128), F32),
            pltpu.VMEM((SIDE, 8, 128), F32),
            pltpu.VMEM((2, 8, BEAMS, 128), BF16),
            pltpu.VMEM((2, SIDE, BEAMS, 128), BF16),
            pltpu.VMEM((2, BEAMS, 128), BF16),
            pltpu.VMEM((2, 8, BEAMS, 128), BF16),
            pltpu.SemaphoreType.DMA((3,)),
            pltpu.SemaphoreType.DMA((9, SIDE)),
            pltpu.SemaphoreType.DMA((9, SIDE)),
        ],
        compiler_params=pltpu.CompilerParams(collective_id=0, has_side_effects=True),
    )(spectra, delays_s, delays_r, wl_index)


def solution(mesh):
    in_specs = (P(None, None, ("row", "col"), None), P("row", None), P("col", None), P())
    out_specs = P(None, None, "col", "row")
    return jax.shard_map(body, mesh=mesh, in_specs=in_specs, out_specs=out_specs, check_vma=False)
```

```python
import functools
import math

import jax
import jax.numpy as jnp
from jax import lax
from jax.experimental import pallas as pl
from jax.experimental.pallas import tpu as pltpu
from jax.sharding import PartitionSpec as P

MESH = pl.DeviceIdType.MESH
F32 = jnp.float32
BF16 = jnp.bfloat16

STATIONS = 10240
WINDOWS = 256
SIDE = 16
OWN = 40
SLOT = 48
HALF = 256
BEAMS = 32
RATES = (0.0361, 0.0596)

COS = (0.9999992215668542, -19.7389825153523, 64.92872658489378, -85.27239662504564, 58.79403695210448, -21.076779298561963)
SIN = (6.283182818541802, -41.34142139793358, 81.59618385577838, -76.58010036540968, 41.20539421297601, -12.271261390344423)

PW, X_ROW, X_COL, LV, SUM_U, SUM_V, ALL_U, ALL_V = range(8)
MARK = 16


def horner(coefs, z):
    acc = jnp.full_like(z, coefs[-1])
    for c in coefs[-2::-1]:
        acc = acc * z + c
    return acc


def kernel(
    spec_hbm, ds_hbm, dr_hbm, wl, out,
    xin, dbuf, tab, turned, pk, xr, xf, pw_send, pw, lv_send, lv, sums, part, block, gathered,
    load, send, recv,
):
    r, c = lax.axis_index("row"), lax.axis_index("col")
    slots = (c // 2, r // 2)
    halves = (c % 2, r % 2)
    holder = (r // 8 == halves[0], c // 8 == halves[1])
    place = (c, r)
    rank = (r, c)

    def peer(axis, other):
        return (r, other) if axis == 0 else (other, c)

    def copy(src, dst, group, device):
        return pltpu.make_async_remote_copy(
            src_ref=src, dst_ref=dst, send_sem=send.at[group], recv_sem=recv.at[group],
            device_id=device, device_id_type=MESH,
        )

    def over_peers(axis, action):
        def step(o, carry):
            action(lax.rem(place[axis] + o, SIDE))
            return carry

        lax.fori_loop(1, SIDE, step, 0)

    def arrived(ref, n, group):
        copy(ref.at[pl.ds(0, n)], ref.at[pl.ds(0, n)], group, (r, c)).wait_recv()

    def left(ref, n, group):
        copy(ref.at[pl.ds(0, n)], ref.at[pl.ds(0, n)], group, (r, c)).wait_send()

    def load_delays(hbm, which):
        start = pl.multiple_of(halves[which] * HALF, HALF)
        return pltpu.make_async_copy(hbm.at[:, pl.ds(start, HALF)], dbuf.at[which], load.at[which])

    loads = [load_delays(ds_hbm, 0), load_delays(dr_hbm, 1)]
    load_x = pltpu.make_async_copy(spec_hbm, xin, load.at[2])
    load_x.start()
    for item in loads:
        item.start()
    barrier = pltpu.get_barrier_semaphore()
    for axis in (0, 1):
        over_peers(axis, lambda p: pl.semaphore_signal(barrier, inc=1, device_id=peer(axis, p), device_id_type=MESH))

    load_x.wait()
    tiles = [[[xin[f, p, :, 128 * t : 128 * t + 128].astype(F32) for t in range(2)] for p in range(2)] for f in range(2)]
    lane = lax.broadcasted_iota(jnp.int32, (8, 128), 1)
    station = (r * SIDE + c) * OWN + lax.broadcasted_iota(jnp.int32, (8, 128), 0)
    power, marked = [], jnp.zeros((8, 128), F32)
    for f in range(2):
        total = sum(tiles[f][p][t] * tiles[f][p][t] for p in range(2) for t in range(2))
        column = jnp.sum(total, axis=1, keepdims=True)
        tile = jnp.zeros((8, 128), F32)
        for j in range(5):
            own = column[8 * j : 8 * j + 8]
            tile = jnp.where(lane == j, own, tile)
            marked = jnp.where((lane == MARK + 5 * f + j) & (station + 8 * j == wl[f]), own, marked)
        power.append(tile)
    for f in range(2):
        pw_send[f] = power[f] + marked

    pl.semaphore_wait(barrier, 2 * (SIDE - 1))

    over_peers(0, lambda p: copy(pw_send.at[p // 8], pw.at[c], PW, peer(0, p)).start())
    pw[c] = pw_send[c // 8]

    low = lax.broadcasted_iota(jnp.int32, (OWN, 128), 1) < 64
    for f in range(2):
        for t in range(2):
            re, im = tiles[f][0][t], tiles[f][1][t]
            first = jnp.where(low, re, pltpu.roll(im, 64, 1))
            second = jnp.where(low, pltpu.roll(re, 64, 1), im)
            for k, value in ((2 * t, first), (2 * t + 1, second)):
                pk[4 * f + k] = jnp.concatenate([value, jnp.zeros((SLOT - OWN, 128), F32)], axis=0).astype(BF16)
    for axis, group in ((1, X_COL), (0, X_ROW)):
        over_peers(axis, lambda p: copy(pk.at[p // 2], xr.at[axis, place[axis]], group, peer(axis, p)).start())
        xr[axis, place[axis]] = pk[place[axis] // 2]

    def steer(which):
        loads[which].wait()
        rate = jnp.where(slots[which] // 4 == 0, RATES[0], RATES[1]).astype(F32)

        def step(q, carry):
            turns = dbuf[which, pl.ds(pl.multiple_of(q * OWN, 8), OWN), :].astype(F32) * rate
            x = turns - jnp.round(turns)
            z = x * x
            pad = jnp.zeros((SLOT - OWN, HALF), F32)
            at = pl.ds(pl.multiple_of(q * SLOT, SLOT), SLOT)
            tab[at, :HALF] = jnp.concatenate([horner(COS, z), pad], axis=0).astype(BF16)
            tab[at, HALF:] = jnp.concatenate([horner(SIN, z) * x, pad], axis=0).astype(BF16)
            return carry

        lax.fori_loop(0, SIDE, step, 0)
        for h in range(2):
            for b in range(SIDE * SLOT // 128):
                turned[which, :, SIDE * SLOT * h + 128 * b : SIDE * SLOT * h + 128 * b + 128] = tab[
                    128 * b : 128 * b + 128, HALF * h : HALF * h + HALF
                ].T

    steer(0)
    arrived(pw, SIDE - 1, PW)
    mark = jnp.where(lane >= MARK, jnp.sum(pw[...], axis=0), 0.0)
    for f in range(2):
        lv_send[f] = jnp.where(lane < MARK, power[f], mark)
    over_peers(1, lambda p: copy(lv_send.at[p // 8], lv.at[r], LV, peer(1, p)).start())
    lv[r] = lv_send[r // 8]
    steer(1)

    low = lax.broadcasted_iota(jnp.int32, (SLOT, 128), 1) < 64
    for axis, group in ((0, X_ROW), (1, X_COL)):
        arrived(xr.at[axis], SIDE - 1, group)

        def unpack(q, carry):
            x = xr[axis, q].astype(F32)
            at = pl.ds(pl.multiple_of(q * SLOT, SLOT), SLOT)
            xf[axis, 0, at] = x
            x = pltpu.roll(x, 64, 1)
            xf[axis, 1, at] = jnp.where(low, -x, x)
            return carry

        lax.fori_loop(0, SIDE, unpack, 0)
    arrived(lv, SIDE - 1, LV)
    mark = jnp.sum(lv[...], axis=0)

    for which, group, source in ((0, SUM_U, pw), (1, SUM_V, lv)):
        start = MARK + 5 * (slots[which] // 4)
        level = 0.5 * jnp.sum(jnp.where((lane >= start) & (lane < start + 5), mark, 0.0), keepdims=True)
        scaled = [[], []]
        for q in range(SIDE):
            gain = lax.rsqrt(source[q] + level)
            gain = jnp.concatenate([gain[:, j : j + 1] for j in range(5)] + [jnp.zeros((8, 1), F32)], axis=0)
            for side in range(2):
                scaled[side].append((xf[which, side, SLOT * q : SLOT * q + SLOT] * gain).astype(BF16))
        value = jnp.dot(
            turned[which], jnp.concatenate(scaled[0] + scaled[1], axis=0), preferred_element_type=F32
        ).astype(BF16)
        for j in range(8):
            sums[which, j] = value[BEAMS * j : BEAMS * j + BEAMS]
        other = 1 - which
        mine = place[other]

        def send_sum(j, carry):
            target = halves[which] * 8 + j

            @pl.when(target != mine)
            def _():
                copy(sums.at[which, j], part.at[which, mine], group, peer(other, target)).start()

            return carry

        lax.fori_loop(0, 8, send_sum, 0)

        @pl.when(holder[which])
        def _():
            part[which, mine] = sums[which, lax.rem(mine, 8)]

    for which, group, after in ((1, SUM_V, ALL_V), (0, SUM_U, ALL_U)):

        @pl.when(holder[which])
        def _():
            arrived(part.at[which], SIDE - 1, group)
            total = jnp.sum(part[which].astype(F32), axis=0).astype(BF16)
            block[which] = total
            over_peers(
                which,
                lambda p: copy(block.at[which], gathered.at[which, slots[which]], after, peer(which, p)).start(),
            )
            gathered[which, slots[which]] = total

    for which, after in ((0, ALL_U), (1, ALL_V)):

        @pl.when(holder[which])
        def _():
            arrived(gathered.at[which], 7, after)

        @pl.when(jnp.logical_not(holder[which]))
        def _():
            arrived(gathered.at[which], 8, after)

    low = lax.broadcasted_iota(jnp.int32, (BEAMS, 128), 1) < 64
    for f in range(2):
        acc = jnp.zeros((BEAMS, 2 * BEAMS), F32)
        for k in range(4):
            u = gathered[0, 4 * f + k]
            swapped = pltpu.roll(u.astype(F32), 64, 1)
            swapped = jnp.where(low, swapped, -swapped).astype(BF16)
            acc += lax.dot_general(
                gathered[1, 4 * f + k], jnp.concatenate([u, swapped], axis=0),
                (((1,), (1,)), ((), ())), preferred_element_type=F32,
            )
        acc = acc * (math.sqrt(WINDOWS) / STATIONS)
        out[f, 0] = acc[:, :BEAMS]
        out[f, 1] = acc[:, BEAMS:]

    left(pw, SIDE - 1, PW)
    left(xr.at[0], SIDE - 1, X_ROW)
    left(xr.at[1], SIDE - 1, X_COL)
    left(lv, SIDE - 1, LV)
    for which, group, after in ((0, SUM_U, ALL_U), (1, SUM_V, ALL_V)):

        @pl.when(holder[which])
        def _():
            left(part.at[which], 7, group)
            left(part.at[which], SIDE - 1, after)

        @pl.when(jnp.logical_not(holder[which]))
        def _():
            left(part.at[which], 8, group)


def body(spectra, delays_s, delays_r, wl_index):
    return pl.pallas_call(
        kernel,
        out_shape=pltpu.VMEM((2, 2, BEAMS, BEAMS), F32),
        in_specs=[pl.BlockSpec(memory_space=pl.ANY)] * 3 + [pl.BlockSpec(memory_space=pltpu.SMEM)],
        out_specs=pl.BlockSpec(memory_space=pltpu.VMEM),
        scratch_shapes=[
            pltpu.VMEM((2, 2, OWN, WINDOWS), BF16),
            pltpu.VMEM((2, SIDE * OWN, HALF), jnp.int32),
            pltpu.VMEM((SIDE * SLOT, 2 * HALF), BF16),
            pltpu.VMEM((2, HALF, 2 * SIDE * SLOT), BF16),
            pltpu.VMEM((8, SLOT, 128), BF16),
            pltpu.VMEM((2, SIDE, SLOT, 128), BF16),
            pltpu.VMEM((2, 2, SIDE * SLOT, 128), F32),
            pltpu.VMEM((2, 8, 128), F32),
            pltpu.VMEM((SIDE, 8, 128), F32),
            pltpu.VMEM((2, 8, 128), F32),
            pltpu.VMEM((SIDE, 8, 128), F32),
            pltpu.VMEM((2, 8, BEAMS, 128), BF16),
            pltpu.VMEM((2, SIDE, BEAMS, 128), BF16),
            pltpu.VMEM((2, BEAMS, 128), BF16),
            pltpu.VMEM((2, 8, BEAMS, 128), BF16),
            pltpu.SemaphoreType.DMA((3,)),
            pltpu.SemaphoreType.DMA((8,)),
            pltpu.SemaphoreType.DMA((8,)),
        ],
        compiler_params=pltpu.CompilerParams(collective_id=0, has_side_effects=True),
    )(spectra, delays_s, delays_r, wl_index)


def solution(mesh):
    in_specs = (P(None, None, ("row", "col"), None), P("row", None), P("col", None), P())
    out_specs = P(None, None, "col", "row")
    return jax.shard_map(body, mesh=mesh, in_specs=in_specs, out_specs=out_specs, check_vma=False)
```

```python
import functools
import math

import jax
import jax.numpy as jnp
from jax import lax
from jax.experimental import pallas as pl
from jax.experimental.pallas import tpu as pltpu
from jax.sharding import PartitionSpec as P

MESH = pl.DeviceIdType.MESH
F32 = jnp.float32
BF16 = jnp.bfloat16

STATIONS = 10240
WINDOWS = 256
SIDE = 16
OWN = 40
SLOT = 48
HALF = 256
BEAMS = 32
RATES = (0.0361, 0.0596)

COS = (0.9999992215668542, -19.7389825153523, 64.92872658489378, -85.27239662504564, 58.79403695210448, -21.076779298561963)
SIN = (6.283182818541802, -41.34142139793358, 81.59618385577838, -76.58010036540968, 41.20539421297601, -12.271261390344423)

PW, X_ROW, X_CORE, X_COL, LV, SUM_U, SUM_V, ALL_U, ALL_V = range(9)
RINGS = ((4, 3, 5, 2, 6, 1, 7, 0), (2, 1, 3, 0))
MARK = OWN


def horner(coefs, z):
    acc = jnp.full_like(z, coefs[-1])
    for c in coefs[-2::-1]:
        acc = acc * z + c
    return acc


def kernel(
    spec_hbm, ds_hbm, dr_hbm, wl, out,
    xin, dbuf, tab, turned, pk, xr, xf, pw_send, pw, powers, lv_send, lv, sums, part, block, gathered, right,
    load, send, recv,
):
    r, c = lax.axis_index("row"), lax.axis_index("col")
    slots = (c // 2, r // 2)
    halves = (c % 2, r % 2)
    holder = (r // 8 == halves[0], c // 8 == halves[1])
    place = (c, r)
    rank = (r, c)

    def peer(axis, other):
        return (r, other) if axis == 0 else (other, c)

    (y_lo, z), (y_hi, x, core) = (r // 8, r % 8), (c // 8, c // 2 % 4, c % 2)
    zs = {d: lax.rem(z + d, 8) for d in RINGS[0]}
    xs = {d: lax.rem(x + d, 4) * 2 for d in RINGS[1]}
    flip = lambda bit, d: 1 - bit if d else bit
    hops = lambda d, n: min(d, n - d)
    others = ([], [])
    for dx, dy, dc in sorted(
        ((dx, dy, dc) for dx in RINGS[1] for dy in (1, 0) for dc in (1, 0)), key=lambda d: -hops(d[0], 4) - 2 * d[1]
    ):
        if dx or dy or dc:
            f = flip(y_hi, dy)
            others[0].append((hops(dx, 4) + 2 * dy, f * 8 + xs[dx] + flip(core, dc), f, f * 4 + lax.div(xs[dx], 2), dc))
    for dz, dy in sorted(((dz, dy) for dz in RINGS[0] for dy in (1, 0)), key=lambda d: -hops(d[0], 8) - d[1]):
        if dz or dy:
            f = flip(y_lo, dy)
            others[1].append((hops(dz, 8) + dy, f * 8 + zs[dz], f, f * 4 + lax.div(zs[dz], 2), 0))

    def copy(src, dst, group, device):
        return pltpu.make_async_remote_copy(
            src_ref=src, dst_ref=dst, send_sem=send.at[group], recv_sem=recv.at[group],
            device_id=device, device_id_type=MESH,
        )

    def arrived(ref, n, group):
        copy(ref.at[pl.ds(0, n)], ref.at[pl.ds(0, n)], group, (r, c)).wait_recv()

    def left(ref, n, group):
        copy(ref.at[pl.ds(0, n)], ref.at[pl.ds(0, n)], group, (r, c)).wait_send()

    def load_delays(hbm, which):
        start = pl.multiple_of(halves[which] * HALF, HALF)
        return pltpu.make_async_copy(hbm.at[:, pl.ds(start, HALF)], dbuf.at[which], load.at[which])

    loads = [load_delays(ds_hbm, 0), load_delays(dr_hbm, 1)]
    load_x = pltpu.make_async_copy(spec_hbm, xin, load.at[2])
    load_x.start()
    for item in loads:
        item.start()
    barrier = pltpu.get_barrier_semaphore()
    for _, axis, p in sorted(((-item[0], axis, k) for axis in (1, 0) for k, item in enumerate(others[axis]))):
        pl.semaphore_signal(barrier, inc=1, device_id=peer(axis, others[axis][p][1]), device_id_type=MESH)

    load_x.wait()
    tiles = [[[xin[f, p, :, 128 * t : 128 * t + 128].astype(F32) for t in range(2)] for p in range(2)] for f in range(2)]
    lane = lax.broadcasted_iota(jnp.int32, (1, 128), 1)
    column = jnp.zeros((OWN, 128), F32)
    for f in range(2):
        total = sum(tiles[f][p][t] * tiles[f][p][t] for p in range(2) for t in range(2))
        at = lax.broadcasted_iota(jnp.int32, (OWN, 128), 1)
        column = jnp.where(at == f, jnp.sum(total, axis=1, keepdims=True), column)
    rows = jnp.concatenate([column, jnp.zeros((128 - OWN, 128), F32)], axis=0).T
    power = [rows[f : f + 1] for f in range(2)]
    station = (r * SIDE + c) * OWN + lane
    marked = jnp.zeros((1, 128), F32)
    for f in range(2):
        mine = (station == wl[f]) & (lane < OWN)
        marked = jnp.where(lane == MARK + f, jnp.sum(jnp.where(mine, power[f], 0.0), axis=1, keepdims=True), marked)
    for f in range(2):
        pw_send[f, :1] = jnp.where(lane < OWN, power[f], marked)

    pl.semaphore_wait(barrier, 2 * (SIDE - 1))

    for _, p, f, _, _ in others[0]:
        copy(pw_send.at[f, pl.ds(0, 1)], pw.at[c, pl.ds(0, 1)], PW, peer(0, p)).start()
    pw[c, :1] = pw_send[c // 8, :1]

    low = lax.broadcasted_iota(jnp.int32, (OWN, 128), 1) < 64
    for f in range(2):
        for t in range(2):
            re, im = tiles[f][0][t], tiles[f][1][t]
            first = jnp.where(low, re, pltpu.roll(im, 64, 1))
            second = jnp.where(low, pltpu.roll(re, 64, 1), im)
            for k, value in ((2 * t, first), (2 * t + 1, second)):
                pk[4 * f + k] = jnp.concatenate([value, jnp.zeros((SLOT - OWN, 128), F32)], axis=0).astype(BF16)
    used = pl.ds(0, OWN)
    at = (core * 8 + c // 2, r)
    for axis, group in ((1, X_COL), (0, X_ROW)):
        for _, p, _, slot, cross in others[axis]:
            if not cross:
                copy(pk.at[slot, used], xr.at[axis, at[axis], used], group, peer(axis, p)).start()
        xr[axis, at[axis]] = pk[place[axis] // 2]

    def steer(which):
        loads[which].wait()
        rate = jnp.where(slots[which] // 4 == 0, RATES[0], RATES[1]).astype(F32)

        def step(q, carry):
            turns = dbuf[which, pl.ds(pl.multiple_of(q * OWN, 8), OWN), :].astype(F32) * rate
            x = turns - jnp.round(turns)
            z = x * x
            pad = jnp.zeros((SLOT - OWN, HALF), F32)
            n = q % 2 * 8 + q // 2 if which == 0 else q
            at = pl.ds(pl.multiple_of(n * SLOT, SLOT), SLOT)
            tab[at, :HALF] = jnp.concatenate([horner(COS, z), pad], axis=0).astype(BF16)
            tab[at, HALF:] = jnp.concatenate([horner(SIN, z) * x, pad], axis=0).astype(BF16)
            return carry

        lax.fori_loop(0, SIDE, step, 0)
        for h in range(2):
            for b in range(SIDE * SLOT // 128):
                turned[which, HALF * h : HALF * h + HALF, 128 * b : 128 * b + 128] = tab[
                    128 * b : 128 * b + 128, HALF * h : HALF * h + HALF
                ].T

    def columns(ref):
        return jnp.concatenate([ref[:, 0, :], jnp.zeros((128 - SIDE, 128), F32)], axis=0).T[:SLOT]

    steer(0)
    arrived(pw.at[:, pl.ds(0, 1)], SIDE - 1, PW)
    mark = jnp.sum(pw[:, 0, :], axis=0, keepdims=True)
    for f in range(2):
        lv_send[f, :1] = jnp.where(lane < OWN, power[f], mark)
    for _, p, f, _, _ in others[1]:
        copy(lv_send.at[f, pl.ds(0, 1)], lv.at[r, pl.ds(0, 1)], LV, peer(1, p)).start()
    lv[r, :1] = lv_send[r // 8, :1]

    arrived(xr.at[0, :, used], 7, X_ROW)
    half = xr.at[0, pl.ds(core * 8, 8), used]
    copy(half, half, X_CORE, peer(0, c + 1 - 2 * core)).start()
    powers[...] = columns(pw)
    steer(1)

    def unpack(axis):
        def step(n, carry):
            at = pl.ds(pl.multiple_of(n * SLOT, SLOT), SLOT)
            xf[axis, at] = jnp.concatenate(
                [xr[axis, n, :OWN].astype(F32), jnp.zeros((SLOT - OWN, 128), F32)], axis=0
            )
            return carry

        lax.fori_loop(0, SIDE, step, 0)

    arrived(xr.at[1, :, used], SIDE - 1, X_COL)
    unpack(1)
    arrived(xr.at[0, :, used], 8, X_CORE)
    unpack(0)
    arrived(lv.at[:, pl.ds(0, 1)], SIDE - 1, LV)
    mark = jnp.sum(lv[:, 0, :], axis=0, keepdims=True)
    station = lax.broadcasted_iota(jnp.int32, (SLOT, 128), 0)
    low = lax.broadcasted_iota(jnp.int32, (HALF, 128), 1) < 64
    for which in range(2):
        level = 0.5 * jnp.sum(jnp.where(lane == MARK + slots[which] // 4, mark, 0.0), axis=1, keepdims=True)
        gain = jnp.where(station < OWN, lax.rsqrt((powers[...] if which == 0 else columns(lv)) + level), 0.0)
        scaled = []
        for n in range(SIDE):
            q = n % 8 * 2 + n // 8 if which == 0 else n
            scaled.append((xf[which, SLOT * n : SLOT * n + SLOT] * gain[:, q : q + 1]).astype(BF16))
        both = jnp.dot(turned[which], jnp.concatenate(scaled, axis=0), preferred_element_type=F32)
        swapped = pltpu.roll(both[HALF:], 64, 1)
        value = (both[:HALF] + jnp.where(low, -swapped, swapped)).astype(BF16)
        for j in range(8):
            sums[which, j] = value[BEAMS * j : BEAMS * j + BEAMS]

    nears = (
        [zs[d] for d in RINGS[0]],
        [xs[d] + flip(core, dc) for d in RINGS[1] for dc in (1, 0)],
    )
    for which, group in ((0, SUM_U), (1, SUM_V)):
        other = 1 - which

        def send_sum(j):
            copy(sums.at[which, j], part.at[which, place[other]], group, peer(other, halves[which] * 8 + j)).start()

        for j in nears[which][:-1]:
            send_sum(j)
        j = nears[which][-1]

        @pl.when(jnp.logical_not(holder[which]))
        def _():
            send_sum(j)

        @pl.when(holder[which])
        def _():
            part[which, place[other]] = sums[which, j]

    for which, group, after in ((1, SUM_V, ALL_V), (0, SUM_U, ALL_U)):

        @pl.when(holder[which])
        def _():
            arrived(part.at[which], SIDE - 1, group)
            total = jnp.sum(part[which].astype(F32), axis=0).astype(BF16)
            block[which] = total
            for _, p, _, _, _ in others[which]:
                copy(block.at[which], gathered.at[which, slots[which]], after, peer(which, p)).start()
            gathered[which, slots[which]] = total

    def all_arrived(which, group):
        @pl.when(holder[which])
        def _():
            arrived(gathered.at[which], 7, group)

        @pl.when(jnp.logical_not(holder[which]))
        def _():
            arrived(gathered.at[which], 8, group)

    all_arrived(0, ALL_U)
    low = lax.broadcasted_iota(jnp.int32, (BEAMS, 128), 1) < 64
    for k in range(8):
        u = gathered[0, k].astype(F32)
        swapped = pltpu.roll(u, 64, 1)
        swapped = jnp.where(low, swapped, -swapped)
        right[k] = jnp.concatenate([u, swapped, jnp.zeros((64, 128), F32)], axis=0).T.astype(BF16)
    all_arrived(1, ALL_V)
    for f in range(2):
        acc = sum(
            jnp.dot(gathered[1, 4 * f + k], right[4 * f + k], preferred_element_type=F32) for k in range(4)
        ) * (math.sqrt(WINDOWS) / STATIONS)
        out[f, 0] = acc[:, :BEAMS]
        out[f, 1] = acc[:, BEAMS : 2 * BEAMS]

    left(pw.at[:, pl.ds(0, 1)], SIDE - 1, PW)
    left(xr.at[0, :, used], 7, X_ROW)
    left(xr.at[0, :, used], 8, X_CORE)
    left(xr.at[1, :, used], SIDE - 1, X_COL)
    left(lv.at[:, pl.ds(0, 1)], SIDE - 1, LV)
    for which, group, after in ((0, SUM_U, ALL_U), (1, SUM_V, ALL_V)):

        @pl.when(holder[which])
        def _():
            left(part.at[which], 7, group)
            left(part.at[which], SIDE - 1, after)

        @pl.when(jnp.logical_not(holder[which]))
        def _():
            left(part.at[which], 8, group)


def body(spectra, delays_s, delays_r, wl_index):
    return pl.pallas_call(
        kernel,
        out_shape=pltpu.VMEM((2, 2, BEAMS, BEAMS), F32),
        in_specs=[pl.BlockSpec(memory_space=pl.ANY)] * 3 + [pl.BlockSpec(memory_space=pltpu.SMEM)],
        out_specs=pl.BlockSpec(memory_space=pltpu.VMEM),
        scratch_shapes=[
            pltpu.VMEM((2, 2, OWN, WINDOWS), BF16),
            pltpu.VMEM((2, SIDE * OWN, HALF), jnp.int32),
            pltpu.VMEM((SIDE * SLOT, 2 * HALF), BF16),
            pltpu.VMEM((2, 2 * HALF, SIDE * SLOT), BF16),
            pltpu.VMEM((8, SLOT, 128), BF16),
            pltpu.VMEM((2, SIDE, SLOT, 128), BF16),
            pltpu.VMEM((2, SIDE * SLOT, 128), F32),
            pltpu.VMEM((2, 8, 128), F32),
            pltpu.VMEM((SIDE, 8, 128), F32),
            pltpu.VMEM((SLOT, 128), F32),
            pltpu.VMEM((2, 8, 128), F32),
            pltpu.VMEM((SIDE, 8, 128), F32),
            pltpu.VMEM((2, 8, BEAMS, 128), BF16),
            pltpu.VMEM((2, SIDE, BEAMS, 128), BF16),
            pltpu.VMEM((2, BEAMS, 128), BF16),
            pltpu.VMEM((2, 8, BEAMS, 128), BF16),
            pltpu.VMEM((8, 128, 128), BF16),
            pltpu.SemaphoreType.DMA((3,)),
            pltpu.SemaphoreType.DMA((9,)),
            pltpu.SemaphoreType.DMA((9,)),
        ],
        compiler_params=pltpu.CompilerParams(collective_id=0, has_side_effects=True),
    )(spectra, delays_s, delays_r, wl_index)


def solution(mesh):
    in_specs = (P(None, None, ("row", "col"), None), P("row", None), P("col", None), P())
    out_specs = P(None, None, "col", "row")
    return jax.shard_map(body, mesh=mesh, in_specs=in_specs, out_specs=out_specs, check_vma=False)
```

```python
import functools
import math

import jax
import jax.numpy as jnp
from jax import lax
from jax.experimental import pallas as pl
from jax.experimental.pallas import tpu as pltpu
from jax.sharding import PartitionSpec as P

MESH = pl.DeviceIdType.MESH
F32 = jnp.float32
BF16 = jnp.bfloat16

STATIONS = 10240
WINDOWS = 256
SIDE = 16
OWN = 40
SLOT = 48
HALF = 256
BEAMS = 32
RATES = (0.0361, 0.0596)

COS = (0.9999992215668542, -19.7389825153523, 64.92872658489378, -85.27239662504564, 58.79403695210448, -21.076779298561963)
SIN = (6.283182818541802, -41.34142139793358, 81.59618385577838, -76.58010036540968, 41.20539421297601, -12.271261390344423)

PW, X_ROW, X_CORE, X_COL, X_FAR, X_HAND, LV, SUM_U, SUM_V, ALL_U, ALL_V = range(11)
RINGS = ((4, 3, 5, 2, 6, 1, 7, 0), (2, 1, 3, 0))
MESSAGE = 3


def horner(coefs, z):
    acc = jnp.full_like(z, coefs[-1])
    for c in coefs[-2::-1]:
        acc = acc * z + c
    return acc


def kernel(
    spec_hbm, ds_hbm, dr_hbm, wl, out,
    xin, dbuf_s, dbuf_r, tab, turned_s, turned_r, pk, xr, xf, pw_send, pw, powers, lv_send, lv, sums_s, sums_r, part, block, gathered, right,
    load, send, recv,
):
    r, c = lax.axis_index("row"), lax.axis_index("col")
    (y_lo, z), (y_hi, x, core) = (r // 8, r % 8), (c // 8, c // 2 % 4, c % 2)
    slots = (c // 2, z)
    halves = (core, 1 - y_lo)
    holder = (core != y_lo, core == y_lo)
    across = (1 - y_lo) * 8 + z

    def peer(axis, other):
        return (r, other) if axis == 0 else (other, c)

    zs = {d: lax.rem(z + d, 8) for d in RINGS[0]}
    xs = {d: lax.rem(x + d, 4) * 2 for d in RINGS[1]}
    flip = lambda bit, d: 1 - bit if d else bit
    hops = lambda d, n: min(d, n - d)
    others, facing = ([], []), []
    for dx, dy, dc in sorted(
        ((dx, dy, dc) for dx in RINGS[1] for dy in (1, 0) for dc in (1, 0)), key=lambda d: -hops(d[0], 4) - 2 * d[1]
    ):
        y = flip(y_hi, dy)
        p = y * 8 + xs[dx] + flip(core, dc)
        if dx or dy or dc:
            others[0].append((hops(dx, 4) + 2 * dy, p, y * 4 + lax.div(xs[dx], 2), dc, False))
        facing.append((hops(dx, 4) + 1, p))
    facing.sort(key=lambda item: -item[0])
    for dz, dy in sorted(((dz, dy) for dz in RINGS[0] for dy in (1, 0)), key=lambda d: -hops(d[0], 8) - d[1]):
        if dz or dy:
            others[1].append((hops(dz, 8) + dy, flip(y_lo, dy) * 8 + zs[dz], zs[dz], dy, hops(dz, 8) > 2))

    def copy(src, dst, group, device):
        return pltpu.make_async_remote_copy(
            src_ref=src, dst_ref=dst, send_sem=send.at[group], recv_sem=recv.at[group],
            device_id=device, device_id_type=MESH,
        )

    def arrived(ref, n, group):
        copy(ref.at[pl.ds(0, n)], ref.at[pl.ds(0, n)], group, (r, c)).wait_recv()

    def left(ref, n, group):
        copy(ref.at[pl.ds(0, n)], ref.at[pl.ds(0, n)], group, (r, c)).wait_send()

    start = pl.multiple_of(halves[0] * HALF, HALF)
    loads = [
        pltpu.make_async_copy(ds_hbm.at[:, pl.ds(start, HALF)], dbuf_s, load.at[0]),
        pltpu.make_async_copy(dr_hbm, dbuf_r, load.at[1]),
    ]
    load_x = pltpu.make_async_copy(spec_hbm, xin, load.at[2])
    load_x.start()
    for item in loads:
        item.start()
    row = pl.ds(0, MESSAGE)
    barrier = pltpu.get_barrier_semaphore()
    plane = [(hop, (r, p)) for hop, p, *_ in others[0]] + [(hop, (across, p)) for hop, p in facing]
    column = [(hop, (p, c)) for hop, p, slot, dy, far in others[1] if not (dy and (far or hop == 1))]
    farthest = lambda devices: [device for _, device in sorted(devices, key=lambda item: -item[0])]
    greeted = farthest(plane + column)
    for device in greeted:
        pl.semaphore_signal(barrier, inc=1, device_id=device, device_id_type=MESH)

    pw_send[...] = jnp.zeros((8, 128), F32)
    load_x.wait()
    tiles = [[[xin[f, p, :, 128 * t : 128 * t + 128].astype(F32) for t in range(2)] for p in range(2)] for f in range(2)]
    lane = lax.broadcasted_iota(jnp.int32, (1, 128), 1)
    column = jnp.zeros((OWN, 128), F32)
    for f in range(2):
        total = sum(tiles[f][p][t] * tiles[f][p][t] for p in range(2) for t in range(2))
        at = lax.broadcasted_iota(jnp.int32, (OWN, 128), 1)
        column = jnp.where(at == f, jnp.sum(total, axis=1, keepdims=True), column)
    rows = jnp.concatenate([column, jnp.zeros((128 - OWN, 128), F32)], axis=0).T
    power = [rows[f : f + 1] for f in range(2)]
    station = (r * SIDE + c) * OWN + lane
    pw_send[:1] = power[0] + pltpu.roll(power[1], OWN, 1)
    for f in range(2):
        mine = (station == wl[f]) & (lane < OWN)
        found = jnp.sum(jnp.where(mine, power[f], 0.0), axis=1, keepdims=True)
        pw_send[1 + f : 2 + f] = jnp.broadcast_to(found, (1, 128))

    pl.semaphore_wait(barrier, len(greeted))

    for device in farthest(plane):
        copy(pw_send.at[row], pw.at[y_lo * SIDE + c, row], PW, device).start()
    pw[y_lo * SIDE + c] = pw_send[...]

    low = lax.broadcasted_iota(jnp.int32, (OWN, 128), 1) < 64
    for f in range(2):
        for t in range(2):
            re, im = tiles[f][0][t], tiles[f][1][t]
            first = jnp.where(low, re, pltpu.roll(im, 64, 1))
            second = jnp.where(low, pltpu.roll(re, 64, 1), im)
            for k, value in ((2 * t, first), (2 * t + 1, second)):
                pk[4 * f + k] = jnp.concatenate([value, jnp.zeros((SLOT - OWN, 128), F32)], axis=0).astype(BF16)
    used = pl.ds(0, OWN)
    for _, p, slot, dy, far in others[1]:
        if not (far and dy):
            copy(pk.at[slot, used], xr.at[1, 8 * dy + z, used], X_FAR if far else X_COL, peer(1, p)).start()
    xr[1, z] = pk[slots[1]]
    for _, p, slot, cross, _ in others[0]:
        if not cross:
            copy(pk.at[slot, used], xr.at[0, core * 8 + c // 2, used], X_ROW, peer(0, p)).start()
    xr[0, core * 8 + c // 2] = pk[slots[0]]

    def steer(which):
        loads[which].wait()
        rate = jnp.where(slots[which] // 4 == 0, RATES[0], RATES[1]).astype(F32)

        def angles(n):
            q = n % 8 * 2 + n // 8 if which == 0 else (y_lo + n // 8) % 2 * 8 + n % 8
            rows = pl.ds(pl.multiple_of(q * OWN, 8), OWN)
            if which == 0:
                delays = dbuf_s[rows]
            else:
                odd = lax.broadcasted_iota(jnp.int32, (OWN, 128), 1) // 32 % 2
                pairs = [[dbuf_r[rows, 256 * t + 128 * a : 256 * t + 128 * a + 128] for a in range(2)] for t in range(2)]
                delays = jnp.concatenate(
                    [jnp.where(odd == halves[1], a, pltpu.roll(b, 32 + 64 * halves[1], 1)) for a, b in pairs], axis=1
                )
            turns = delays.astype(F32) * rate
            return turns - jnp.round(turns)

        def step(m, carry):
            x = jnp.concatenate([angles(2 * m), angles(2 * m + 1)], axis=0)
            z = x * x
            at = pl.ds(pl.multiple_of(m * 2 * OWN, 2 * OWN), 2 * OWN)
            tab[at, :HALF] = horner(COS, z).astype(BF16)
            tab[at, HALF:] = (horner(SIN, z) * x).astype(BF16)
            return carry

        lax.fori_loop(0, SIDE // 2, step, 0)
        for h in range(2):
            for b in range(SIDE * OWN // 128):
                value = tab[128 * b : 128 * b + 128, HALF * h : HALF * h + HALF].T
                if which == 0:
                    turned_s[HALF * h : HALF * h + HALF, 128 * b : 128 * b + 128] = value
                else:
                    turned_r[:, SIDE * OWN * h + 128 * b : SIDE * OWN * h + 128 * b + 128] = value

    def columns(rows):
        return jnp.concatenate([rows, jnp.zeros((128 - rows.shape[0], 128), F32)], axis=0).T

    steer(0)
    arrived(pw.at[:, row], 2 * SIDE - 1, PW)
    plane_sum = jnp.sum(pw[...], axis=0)
    there = pw[(1 - y_lo) * SIDE + c, :1]
    first = lax.broadcasted_iota(jnp.int32, (8, 128), 0) == 0
    for f in range(2):
        both = jnp.where(lane < OWN, power[f], there if f else pltpu.roll(there, OWN, 1))
        lv_send[f] = jnp.where(first, both, plane_sum)
    for _, p, slot, dy, _ in others[1]:
        if not dy:
            copy(lv_send.at[lax.div(slot, 4), row], lv.at[z, row], LV, peer(1, p)).start()
    lv[z] = lv_send[z // 4]

    arrived(xr.at[1, :, used], 3, X_FAR)
    for d in (4, 3, 5):
        copy(xr.at[1, zs[d], used], xr.at[1, 8 + zs[d], used], X_HAND, (across, c)).start()
    arrived(xr.at[0, :, used], 7, X_ROW)
    half = xr.at[0, pl.ds(core * 8, 8), used]
    copy(half, half, X_CORE, peer(0, c + 1 - 2 * core)).start()
    here = pw[pl.ds(y_lo * SIDE, SIDE), 0, :]
    powers[...] = columns(jnp.where(y_hi == 0, here, pltpu.roll(here, 128 - OWN, 1)))[:OWN]
    steer(1)

    low_x = lax.broadcasted_iota(jnp.int32, (OWN, 128), 1) < 64

    def unpack(axis):
        def step(n, carry):
            value = xr[axis, n, :OWN].astype(F32)
            xf[axis, pl.ds(pl.multiple_of(n * OWN, 8), OWN)] = value
            if axis == 1:
                value = pltpu.roll(value, 64, 1)
                xf[2, pl.ds(pl.multiple_of(n * OWN, 8), OWN)] = jnp.where(low_x, -value, value)
            return carry

        lax.fori_loop(0, SIDE, step, 0)

    arrived(xr.at[0, :, used], 8, X_CORE)
    unpack(0)
    arrived(xr.at[1, :, used], 9, X_COL)
    arrived(xr.at[1, :, used], 3, X_HAND)
    unpack(1)
    arrived(lv.at[:, row], 7, LV)
    marks = 0.5 * jnp.sum(lv[...], axis=0)
    level = [jnp.where(slots[which] // 4 == 0, marks[1:2], marks[2:3]) for which in range(2)]

    gain = lax.rsqrt(powers[...] + level[0])
    scaled = [
        xf[0, OWN * n : OWN * n + OWN] * gain[:, n % 8 * 2 + n // 8 : n % 8 * 2 + n // 8 + 1] for n in range(SIDE)
    ]
    both = jnp.dot(turned_s[...], jnp.concatenate(scaled, axis=0).astype(BF16), preferred_element_type=F32)
    low = lax.broadcasted_iota(jnp.int32, (HALF, 128), 1) < 64
    swapped = pltpu.roll(both[HALF:], 64, 1)
    value = (both[:HALF] + jnp.where(low, -swapped, swapped)).astype(BF16)
    for j in range(8):
        sums_s[j] = value[BEAMS * j : BEAMS * j + BEAMS]
    for d in RINGS[0][:-1]:
        copy(sums_s.at[zs[d]], part.at[0, r], SUM_U, peer(1, (1 - core) * 8 + zs[d])).start()

    gain = lax.rsqrt(columns(lv[:, 0, :])[: 2 * OWN] + level[1])
    scaled = []
    for side in (1, 2):
        for n in range(SIDE):
            own = gain[n // 8 * OWN : n // 8 * OWN + OWN, n % 8 : n % 8 + 1]
            scaled.append(xf[side, OWN * n : OWN * n + OWN] * own)
    value = jnp.dot(
        turned_r[...], jnp.concatenate(scaled, axis=0).astype(BF16), preferred_element_type=F32
    ).astype(BF16)
    for j in range(8):
        sums_r[j] = value[BEAMS * j : BEAMS * j + BEAMS]
    for dx, dy in ((dx, dy) for dx in RINGS[1] for dy in (1, 0)):
        y, xx, h = flip(y_hi, dy), lax.div(xs[dx], 2), halves[1]
        a = lax.div(xx, 2)
        j = 4 * y + 2 * lax.rem(xx, 2) + a + h - 2 * a * h
        copy(sums_r.at[j], part.at[1, c], SUM_V, (across, y * 8 + xs[dx] + h)).start()

    @pl.when(jnp.logical_not(holder[0]))
    def _():
        copy(sums_s.at[z], part.at[0, r], SUM_U, peer(1, across)).start()

    @pl.when(holder[0])
    def _():
        part[0, r] = sums_s[z]

    def total(which):
        value = jnp.sum(part[which].astype(F32), axis=0).astype(BF16)
        block[which] = value
        return value

    @pl.when(holder[1])
    def _():
        arrived(part.at[1], SIDE, SUM_V)
        value = total(1)
        for _, p, *_ in others[1]:
            copy(block.at[1], gathered.at[1, z], ALL_V, peer(1, p)).start()
        gathered[1, z] = value

    @pl.when(holder[0])
    def _():
        arrived(part.at[0], SIDE - 1, SUM_U)
        total(0)
        for _, p in facing:
            copy(block.at[0], gathered.at[0, slots[0]], ALL_U, (across, p)).start()

    arrived(gathered.at[0], 8, ALL_U)
    low = lax.broadcasted_iota(jnp.int32, (BEAMS, 128), 1) < 64
    for k in range(8):
        u = gathered[0, k].astype(F32)
        swapped = pltpu.roll(u, 64, 1)
        swapped = jnp.where(low, swapped, -swapped)
        right[k // 4, 128 * (k % 4) : 128 * (k % 4) + 128] = jnp.concatenate(
            [u, swapped, jnp.zeros((64, 128), F32)], axis=0
        ).T.astype(BF16)
    left(pw.at[:, row], 2 * SIDE - 1, PW)
    left(xr.at[0, :, used], 7, X_ROW)
    left(xr.at[0, :, used], 8, X_CORE)
    left(xr.at[1, :, used], 9, X_COL)
    left(xr.at[1, :, used], 3, X_FAR)
    left(xr.at[1, :, used], 3, X_HAND)
    left(lv.at[:, row], 7, LV)
    left(part.at[1], 8, SUM_V)

    @pl.when(holder[0])
    def _():
        left(part.at[0], 7, SUM_U)
        left(part.at[0], SIDE, ALL_U)
        arrived(gathered.at[1], 8, ALL_V)

    @pl.when(holder[1])
    def _():
        left(part.at[0], 8, SUM_U)
        left(part.at[1], SIDE - 1, ALL_V)
        arrived(gathered.at[1], 7, ALL_V)

    for f in range(2):
        v = jnp.concatenate([gathered[1, 4 * f + k] for k in range(4)], axis=1)
        value = jnp.dot(v, right[f], preferred_element_type=F32) * (math.sqrt(WINDOWS) / STATIONS)
        out[f, 0] = value[:, :BEAMS]
        out[f, 1] = value[:, BEAMS : 2 * BEAMS]


def body(spectra, delays_s, delays_r, wl_index):
    return pl.pallas_call(
        kernel,
        out_shape=pltpu.VMEM((2, 2, BEAMS, BEAMS), F32),
        in_specs=[pl.BlockSpec(memory_space=pl.ANY)] * 3 + [pl.BlockSpec(memory_space=pltpu.SMEM)],
        out_specs=pl.BlockSpec(memory_space=pltpu.VMEM),
        scratch_shapes=[
            pltpu.VMEM((2, 2, OWN, WINDOWS), BF16),
            pltpu.VMEM((SIDE * OWN, HALF), jnp.int32),
            pltpu.VMEM((SIDE * OWN, 2 * HALF), jnp.int32),
            pltpu.VMEM((SIDE * OWN, 2 * HALF), BF16),
            pltpu.VMEM((2 * HALF, SIDE * OWN), BF16),
            pltpu.VMEM((HALF, 2 * SIDE * OWN), BF16),
            pltpu.VMEM((8, SLOT, 128), BF16),
            pltpu.VMEM((2, SIDE, SLOT, 128), BF16),
            pltpu.VMEM((3, SIDE * OWN, 128), F32),
            pltpu.VMEM((8, 128), F32),
            pltpu.VMEM((2 * SIDE, 8, 128), F32),
            pltpu.VMEM((OWN, 128), F32),
            pltpu.VMEM((2, 8, 128), F32),
            pltpu.VMEM((8, 8, 128), F32),
            pltpu.VMEM((8, BEAMS, 128), BF16),
            pltpu.VMEM((8, BEAMS, 128), BF16),
            pltpu.VMEM((2, SIDE, BEAMS, 128), BF16),
            pltpu.VMEM((2, BEAMS, 128), BF16),
            pltpu.VMEM((2, 8, BEAMS, 128), BF16),
            pltpu.VMEM((2, 512, 128), BF16),
            pltpu.SemaphoreType.DMA((3,)),
            pltpu.SemaphoreType.DMA((11,)),
            pltpu.SemaphoreType.DMA((11,)),
        ],
        compiler_params=pltpu.CompilerParams(collective_id=0, has_side_effects=True),
    )(spectra, delays_s, delays_r, wl_index)


def solution(mesh):
    in_specs = (P(None, None, ("row", "col"), None), P("row", None), P("col", None), P())
    out_specs = P(None, None, "col", "row")
    return jax.shard_map(body, mesh=mesh, in_specs=in_specs, out_specs=out_specs, check_vma=False)
```

```python
import functools
import math

import jax
import jax.numpy as jnp
from jax import lax
from jax.experimental import pallas as pl
from jax.experimental.pallas import tpu as pltpu
from jax.sharding import PartitionSpec as P

MESH = pl.DeviceIdType.MESH
F32 = jnp.float32
BF16 = jnp.bfloat16

STATIONS = 10240
WINDOWS = 256
SIDE = 16
OWN = 40
SLOT = 48
HALF = 256
BEAMS = 32
RATES = (0.0361, 0.0596)

COS = (0.9999992215668542, -19.7389825153523, 64.92872658489378, -85.27239662504564, 58.79403695210448, -21.076779298561963)
SIN = (6.283182818541802, -41.34142139793358, 81.59618385577838, -76.58010036540968, 41.20539421297601, -12.271261390344423)

PW, X_ROW, X_CORE, X_COL, X_FAR, X_HAND, LV, SUM_U, SUM_V, ALL_U, ALL_V = range(11)
RINGS = ((4, 3, 5, 2, 6, 1, 7, 0), (2, 1, 3, 0))
MESSAGE = 3


def horner(coefs, z):
    acc = jnp.full_like(z, coefs[-1])
    for c in coefs[-2::-1]:
        acc = acc * z + c
    return acc


def kernel(
    spec_hbm, ds_hbm, dr_hbm, wl, out,
    xin, dbuf_s, dbuf_r, tab, turned_s, turned_r, pk, xr, xf, pw_send, pw, powers, lv_send, lv, sums_s, sums_r, part, block, gathered, right,
    load, send, recv,
):
    r, c = lax.axis_index("row"), lax.axis_index("col")
    (y_lo, z), (y_hi, x, core) = (r // 8, r % 8), (c // 8, c // 2 % 4, c % 2)
    slots = (c // 2, z)
    halves = (core, 1 - y_lo)
    holder = (core != y_lo, core == y_lo)
    across = (1 - y_lo) * 8 + z

    def peer(axis, other):
        return (r, other) if axis == 0 else (other, c)

    zs = {d: lax.rem(z + d, 8) for d in RINGS[0]}
    xs = {d: lax.rem(x + d, 4) * 2 for d in RINGS[1]}
    flip = lambda bit, d: 1 - bit if d else bit
    hops = lambda d, n: min(d, n - d)
    others, facing = ([], []), []
    for dx, dy, dc in sorted(
        ((dx, dy, dc) for dx in RINGS[1] for dy in (1, 0) for dc in (1, 0)), key=lambda d: -hops(d[0], 4) - 2 * d[1]
    ):
        y = flip(y_hi, dy)
        p = y * 8 + xs[dx] + flip(core, dc)
        if dx or dy or dc:
            others[0].append((hops(dx, 4) + 2 * dy, p, y * 4 + lax.div(xs[dx], 2), dc, False))
        facing.append((hops(dx, 4) + 1, p))
    facing.sort(key=lambda item: -item[0])
    for dz, dy in sorted(((dz, dy) for dz in RINGS[0] for dy in (1, 0)), key=lambda d: -hops(d[0], 8) - d[1]):
        if dz or dy:
            others[1].append((hops(dz, 8) + dy, flip(y_lo, dy) * 8 + zs[dz], zs[dz], dy, hops(dz, 8) > 2))

    def copy(src, dst, group, device):
        return pltpu.make_async_remote_copy(
            src_ref=src, dst_ref=dst, send_sem=send.at[group], recv_sem=recv.at[group],
            device_id=device, device_id_type=MESH,
        )

    def arrived(ref, n, group):
        copy(ref.at[pl.ds(0, n)], ref.at[pl.ds(0, n)], group, (r, c)).wait_recv()

    def left(ref, n, group):
        copy(ref.at[pl.ds(0, n)], ref.at[pl.ds(0, n)], group, (r, c)).wait_send()

    start = pl.multiple_of(halves[0] * HALF, HALF)
    loads = [
        pltpu.make_async_copy(ds_hbm.at[:, pl.ds(start, HALF)], dbuf_s, load.at[0]),
        pltpu.make_async_copy(dr_hbm, dbuf_r, load.at[1]),
    ]
    load_x = pltpu.make_async_copy(spec_hbm, xin, load.at[2])
    load_x.start()
    for item in loads:
        item.start()
    row = pl.ds(0, MESSAGE)
    barrier = pltpu.get_barrier_semaphore()
    plane = [(hop, (r, p)) for hop, p, *_ in others[0]] + [(hop, (across, p)) for hop, p in facing]
    column = [(hop, (p, c)) for hop, p, slot, dy, far in others[1] if not (dy and (far or hop == 1))]
    farthest = lambda devices: [device for _, device in sorted(devices, key=lambda item: -item[0])]
    greeted = farthest(plane + column)
    for device in greeted:
        pl.semaphore_signal(barrier, inc=1, device_id=device, device_id_type=MESH)

    pw_send[...] = jnp.zeros((8, 128), F32)
    load_x.wait()
    tiles = [[[xin[f, p, :, 128 * t : 128 * t + 128].astype(F32) for t in range(2)] for p in range(2)] for f in range(2)]
    lane = lax.broadcasted_iota(jnp.int32, (1, 128), 1)
    column = jnp.zeros((OWN, 128), F32)
    for f in range(2):
        total = sum(tiles[f][p][t] * tiles[f][p][t] for p in range(2) for t in range(2))
        at = lax.broadcasted_iota(jnp.int32, (OWN, 128), 1)
        column = jnp.where(at == f, jnp.sum(total, axis=1, keepdims=True), column)
    rows = jnp.concatenate([column, jnp.zeros((128 - OWN, 128), F32)], axis=0).T
    power = [rows[f : f + 1] for f in range(2)]
    station = (r * SIDE + c) * OWN + lane
    pw_send[:1] = power[0] + pltpu.roll(power[1], OWN, 1)
    for f in range(2):
        mine = (station == wl[f]) & (lane < OWN)
        found = jnp.sum(jnp.where(mine, power[f], 0.0), axis=1, keepdims=True)
        pw_send[1 + f : 2 + f] = jnp.broadcast_to(found, (1, 128))

    pl.semaphore_wait(barrier, len(greeted))

    for device in farthest(plane):
        copy(pw_send.at[row], pw.at[y_lo * SIDE + c, row], PW, device).start()
    pw[y_lo * SIDE + c] = pw_send[...]

    low = lax.broadcasted_iota(jnp.int32, (OWN, 128), 1) < 64
    for f in range(2):
        for t in range(2):
            re, im = tiles[f][0][t], tiles[f][1][t]
            first = jnp.where(low, re, pltpu.roll(im, 64, 1))
            second = jnp.where(low, pltpu.roll(re, 64, 1), im)
            for k, value in ((2 * t, first), (2 * t + 1, second)):
                pk[4 * f + k] = jnp.concatenate([value, jnp.zeros((SLOT - OWN, 128), F32)], axis=0).astype(BF16)
    used = pl.ds(0, OWN)
    for _, p, slot, dy, far in sorted(others[1], key=lambda item: not item[4]):
        if not (far and dy):
            copy(pk.at[slot, used], xr.at[1, 8 * dy + z, used], X_FAR if far else X_COL, peer(1, p)).start()
    xr[1, z] = pk[slots[1]]
    for _, p, slot, cross, _ in others[0]:
        if not cross:
            copy(pk.at[slot, used], xr.at[0, core * 8 + c // 2, used], X_ROW, peer(0, p)).start()
    xr[0, core * 8 + c // 2] = pk[slots[0]]

    def steer(which):
        loads[which].wait()
        rate = jnp.where(slots[which] // 4 == 0, RATES[0], RATES[1]).astype(F32)

        def angles(n):
            q = n % 8 * 2 + n // 8 if which == 0 else (y_lo + n // 8) % 2 * 8 + n % 8
            rows = pl.ds(pl.multiple_of(q * OWN, 8), OWN)
            if which == 0:
                delays = dbuf_s[rows]
            else:
                odd = lax.broadcasted_iota(jnp.int32, (OWN, 128), 1) // 32 % 2
                pairs = [[dbuf_r[rows, 256 * t + 128 * a : 256 * t + 128 * a + 128] for a in range(2)] for t in range(2)]
                delays = jnp.concatenate(
                    [jnp.where(odd == halves[1], a, pltpu.roll(b, 32 + 64 * halves[1], 1)) for a, b in pairs], axis=1
                )
            turns = delays.astype(F32) * rate
            return turns - jnp.round(turns)

        def step(m, carry):
            x = jnp.concatenate([angles(2 * m), angles(2 * m + 1)], axis=0)
            z = x * x
            at = pl.ds(pl.multiple_of(m * 2 * OWN, 2 * OWN), 2 * OWN)
            tab[at, :HALF] = horner(COS, z).astype(BF16)
            tab[at, HALF:] = (horner(SIN, z) * x).astype(BF16)
            return carry

        lax.fori_loop(0, SIDE // 2, step, 0)
        for h in range(2):
            for b in range(SIDE * OWN // 128):
                value = tab[128 * b : 128 * b + 128, HALF * h : HALF * h + HALF].T
                if which == 0:
                    turned_s[HALF * h : HALF * h + HALF, 128 * b : 128 * b + 128] = value
                else:
                    turned_r[:, SIDE * OWN * h + 128 * b : SIDE * OWN * h + 128 * b + 128] = value

    def columns(rows):
        return jnp.concatenate([rows, jnp.zeros((128 - rows.shape[0], 128), F32)], axis=0).T

    steer(0)
    arrived(pw.at[:, row], 2 * SIDE - 1, PW)
    plane_sum = jnp.sum(pw[...], axis=0)
    there = pw[(1 - y_lo) * SIDE + c, :1]
    first = lax.broadcasted_iota(jnp.int32, (8, 128), 0) == 0
    for f in range(2):
        both = jnp.where(lane < OWN, power[f], there if f else pltpu.roll(there, OWN, 1))
        lv_send[f] = jnp.where(first, both, plane_sum)
    for _, p, slot, dy, _ in others[1]:
        if not dy:
            copy(lv_send.at[lax.div(slot, 4), row], lv.at[z, row], LV, peer(1, p)).start()
    lv[z] = lv_send[z // 4]

    arrived(xr.at[1, :, used], 3, X_FAR)
    for d in (4, 3, 5):
        copy(xr.at[1, zs[d], used], xr.at[1, 8 + zs[d], used], X_HAND, (across, c)).start()
    arrived(xr.at[0, :, used], 7, X_ROW)
    half = xr.at[0, pl.ds(core * 8, 8), used]
    copy(half, half, X_CORE, peer(0, c + 1 - 2 * core)).start()
    here = pw[pl.ds(y_lo * SIDE, SIDE), 0, :]
    powers[...] = columns(jnp.where(y_hi == 0, here, pltpu.roll(here, 128 - OWN, 1)))[:OWN]
    steer(1)

    low_x = lax.broadcasted_iota(jnp.int32, (OWN, 128), 1) < 64

    def unpack(axis, start, stop):
        def step(i, carry):
            n = i if axis == 0 else i // 8 * 8 + (z + 6 + i) % 8
            value = xr[axis, n, :OWN].astype(F32)
            xf[axis, pl.ds(pl.multiple_of(n * OWN, 8), OWN)] = value
            if axis == 1:
                value = pltpu.roll(value, 64, 1)
                xf[2, pl.ds(pl.multiple_of(n * OWN, 8), OWN)] = jnp.where(low_x, -value, value)
            return carry

        lax.fori_loop(start, stop, step, 0)

    arrived(xr.at[0, :, used], 8, X_CORE)
    unpack(0, 0, SIDE)
    arrived(xr.at[1, :, used], 9, X_COL)
    unpack(1, 0, SIDE - 3)
    arrived(xr.at[1, :, used], 3, X_HAND)
    unpack(1, SIDE - 3, SIDE)
    arrived(lv.at[:, row], 7, LV)
    marks = 0.5 * jnp.sum(lv[...], axis=0)
    level = [jnp.where(slots[which] // 4 == 0, marks[1:2], marks[2:3]) for which in range(2)]

    gain = lax.rsqrt(powers[...] + level[0])
    scaled = [
        xf[0, OWN * n : OWN * n + OWN] * gain[:, n % 8 * 2 + n // 8 : n % 8 * 2 + n // 8 + 1] for n in range(SIDE)
    ]
    both = jnp.dot(turned_s[...], jnp.concatenate(scaled, axis=0).astype(BF16), preferred_element_type=F32)
    low = lax.broadcasted_iota(jnp.int32, (HALF, 128), 1) < 64
    swapped = pltpu.roll(both[HALF:], 64, 1)
    value = (both[:HALF] + jnp.where(low, -swapped, swapped)).astype(BF16)
    for j in range(8):
        sums_s[j] = value[BEAMS * j : BEAMS * j + BEAMS]
    for d in RINGS[0][:-1]:
        copy(sums_s.at[zs[d]], part.at[0, r], SUM_U, peer(1, (1 - core) * 8 + zs[d])).start()

    gain = lax.rsqrt(columns(lv[:, 0, :])[: 2 * OWN] + level[1])
    scaled = []
    for side in (1, 2):
        for n in range(SIDE):
            own = gain[n // 8 * OWN : n // 8 * OWN + OWN, n % 8 : n % 8 + 1]
            scaled.append(xf[side, OWN * n : OWN * n + OWN] * own)
    value = jnp.dot(
        turned_r[...], jnp.concatenate(scaled, axis=0).astype(BF16), preferred_element_type=F32
    ).astype(BF16)
    for j in range(8):
        sums_r[j] = value[BEAMS * j : BEAMS * j + BEAMS]
    for dx, dy in ((dx, dy) for dx in RINGS[1] for dy in (1, 0)):
        y, xx, h = flip(y_hi, dy), lax.div(xs[dx], 2), halves[1]
        a = lax.div(xx, 2)
        j = 4 * y + 2 * lax.rem(xx, 2) + a + h - 2 * a * h
        copy(sums_r.at[j], part.at[1, c], SUM_V, (across, y * 8 + xs[dx] + h)).start()

    @pl.when(jnp.logical_not(holder[0]))
    def _():
        copy(sums_s.at[z], part.at[0, r], SUM_U, peer(1, across)).start()

    @pl.when(holder[0])
    def _():
        part[0, r] = sums_s[z]

    def total(which):
        value = jnp.sum(part[which].astype(F32), axis=0).astype(BF16)
        block[which] = value
        return value

    @pl.when(holder[1])
    def _():
        arrived(part.at[1], SIDE, SUM_V)
        value = total(1)
        for _, p, *_ in others[1]:
            copy(block.at[1], gathered.at[1, z], ALL_V, peer(1, p)).start()
        gathered[1, z] = value

    @pl.when(holder[0])
    def _():
        arrived(part.at[0], SIDE - 1, SUM_U)
        total(0)
        for _, p in facing:
            copy(block.at[0], gathered.at[0, slots[0]], ALL_U, (across, p)).start()

    arrived(gathered.at[0], 8, ALL_U)
    low = lax.broadcasted_iota(jnp.int32, (BEAMS, 128), 1) < 64
    for k in range(8):
        u = gathered[0, k].astype(F32)
        swapped = pltpu.roll(u, 64, 1)
        swapped = jnp.where(low, swapped, -swapped)
        right[k // 4, 128 * (k % 4) : 128 * (k % 4) + 128] = jnp.concatenate(
            [u, swapped, jnp.zeros((64, 128), F32)], axis=0
        ).T.astype(BF16)
    left(pw.at[:, row], 2 * SIDE - 1, PW)
    left(xr.at[0, :, used], 7, X_ROW)
    left(xr.at[0, :, used], 8, X_CORE)
    left(xr.at[1, :, used], 9, X_COL)
    left(xr.at[1, :, used], 3, X_FAR)
    left(xr.at[1, :, used], 3, X_HAND)
    left(lv.at[:, row], 7, LV)
    left(part.at[1], 8, SUM_V)

    @pl.when(holder[0])
    def _():
        left(part.at[0], 7, SUM_U)
        left(part.at[0], SIDE, ALL_U)
        arrived(gathered.at[1], 8, ALL_V)

    @pl.when(holder[1])
    def _():
        left(part.at[0], 8, SUM_U)
        left(part.at[1], SIDE - 1, ALL_V)
        arrived(gathered.at[1], 7, ALL_V)

    for f in range(2):
        v = jnp.concatenate([gathered[1, 4 * f + k] for k in range(4)], axis=1)
        value = jnp.dot(v, right[f], preferred_element_type=F32) * (math.sqrt(WINDOWS) / STATIONS)
        out[f, 0] = value[:, :BEAMS]
        out[f, 1] = value[:, BEAMS : 2 * BEAMS]


def body(spectra, delays_s, delays_r, wl_index):
    return pl.pallas_call(
        kernel,
        out_shape=pltpu.VMEM((2, 2, BEAMS, BEAMS), F32),
        in_specs=[pl.BlockSpec(memory_space=pl.ANY)] * 3 + [pl.BlockSpec(memory_space=pltpu.SMEM)],
        out_specs=pl.BlockSpec(memory_space=pltpu.VMEM),
        scratch_shapes=[
            pltpu.VMEM((2, 2, OWN, WINDOWS), BF16),
            pltpu.VMEM((SIDE * OWN, HALF), jnp.int32),
            pltpu.VMEM((SIDE * OWN, 2 * HALF), jnp.int32),
            pltpu.VMEM((SIDE * OWN, 2 * HALF), BF16),
            pltpu.VMEM((2 * HALF, SIDE * OWN), BF16),
            pltpu.VMEM((HALF, 2 * SIDE * OWN), BF16),
            pltpu.VMEM((8, SLOT, 128), BF16),
            pltpu.VMEM((2, SIDE, SLOT, 128), BF16),
            pltpu.VMEM((3, SIDE * OWN, 128), F32),
            pltpu.VMEM((8, 128), F32),
            pltpu.VMEM((2 * SIDE, 8, 128), F32),
            pltpu.VMEM((OWN, 128), F32),
            pltpu.VMEM((2, 8, 128), F32),
            pltpu.VMEM((8, 8, 128), F32),
            pltpu.VMEM((8, BEAMS, 128), BF16),
            pltpu.VMEM((8, BEAMS, 128), BF16),
            pltpu.VMEM((2, SIDE, BEAMS, 128), BF16),
            pltpu.VMEM((2, BEAMS, 128), BF16),
            pltpu.VMEM((2, 8, BEAMS, 128), BF16),
            pltpu.VMEM((2, 512, 128), BF16),
            pltpu.SemaphoreType.DMA((3,)),
            pltpu.SemaphoreType.DMA((11,)),
            pltpu.SemaphoreType.DMA((11,)),
        ],
        compiler_params=pltpu.CompilerParams(collective_id=0, has_side_effects=True),
    )(spectra, delays_s, delays_r, wl_index)


def solution(mesh):
    in_specs = (P(None, None, ("row", "col"), None), P("row", None), P("col", None), P())
    out_specs = P(None, None, "col", "row")
    return jax.shard_map(body, mesh=mesh, in_specs=in_specs, out_specs=out_specs, check_vma=False)
```

```python
import functools
import math

import jax
import jax.numpy as jnp
from jax import lax
from jax.experimental import pallas as pl
from jax.experimental.pallas import tpu as pltpu
from jax.sharding import PartitionSpec as P

MESH = pl.DeviceIdType.MESH
F32 = jnp.float32
BF16 = jnp.bfloat16

STATIONS = 10240
WINDOWS = 256
SIDE = 16
OWN = 40
SLOT = 48
HALF = 256
BEAMS = 32
RATES = (0.0361, 0.0596)

COS = (0.9999992215668542, -19.7389825153523, 64.92872658489378, -85.27239662504564, 58.79403695210448, -21.076779298561963)
SIN = (6.283182818541802, -41.34142139793358, 81.59618385577838, -76.58010036540968, 41.20539421297601, -12.271261390344423)

PW, X_ROW, X_CORE, X_COL, X_FAR, X_HAND, LV, SUM_U, SUM_V, ALL_U, ALL_V = range(11)
RINGS = ((4, 3, 5, 2, 6, 1, 7, 0), (2, 1, 3, 0))
MESSAGE = 3


def horner(coefs, z):
    acc = jnp.full_like(z, coefs[-1])
    for c in coefs[-2::-1]:
        acc = acc * z + c
    return acc


def kernel(
    spec_hbm, ds_hbm, dr_hbm, wl, out,
    xin, dbuf_s, dbuf_r, tab, turned_s, turned_r, pk, xr, xf, pw_send, pw, powers, lv_send, lv, sums_s, sums_r, part, block, gathered, right,
    load, send, recv,
):
    r, c = lax.axis_index("row"), lax.axis_index("col")
    (y_lo, z), (y_hi, x, core) = (r // 8, r % 8), (c // 8, c // 2 % 4, c % 2)
    slots = (c // 2, z)
    halves = (core, 1 - y_lo)
    holder = (core != y_lo, core == y_lo)
    across = (1 - y_lo) * 8 + z

    def peer(axis, other):
        return (r, other) if axis == 0 else (other, c)

    zs = {d: lax.rem(z + d, 8) for d in RINGS[0]}
    xs = {d: lax.rem(x + d, 4) * 2 for d in RINGS[1]}
    flip = lambda bit, d: 1 - bit if d else bit
    hops = lambda d, n: min(d, n - d)
    others, facing = ([], []), []
    for dx, dy, dc in sorted(
        ((dx, dy, dc) for dx in RINGS[1] for dy in (1, 0) for dc in (1, 0)), key=lambda d: -hops(d[0], 4) - 2 * d[1]
    ):
        y = flip(y_hi, dy)
        p = y * 8 + xs[dx] + flip(core, dc)
        if dx or dy or dc:
            others[0].append((hops(dx, 4) + 2 * dy, p, y * 4 + lax.div(xs[dx], 2), dc, False))
        facing.append((hops(dx, 4) + 1, p))
    facing.sort(key=lambda item: -item[0])
    for dz, dy in sorted(((dz, dy) for dz in RINGS[0] for dy in (1, 0)), key=lambda d: -hops(d[0], 8) - d[1]):
        if dz or dy:
            others[1].append((hops(dz, 8) + dy, flip(y_lo, dy) * 8 + zs[dz], zs[dz], dy, hops(dz, 8) > 2))

    def copy(src, dst, group, device):
        return pltpu.make_async_remote_copy(
            src_ref=src, dst_ref=dst, send_sem=send.at[group], recv_sem=recv.at[group],
            device_id=device, device_id_type=MESH,
        )

    def arrived(ref, n, group):
        copy(ref.at[pl.ds(0, n)], ref.at[pl.ds(0, n)], group, (r, c)).wait_recv()

    def left(ref, n, group):
        copy(ref.at[pl.ds(0, n)], ref.at[pl.ds(0, n)], group, (r, c)).wait_send()

    start = pl.multiple_of(halves[0] * HALF, HALF)
    loads = [
        pltpu.make_async_copy(ds_hbm.at[:, pl.ds(start, HALF)], dbuf_s, load.at[0]),
        pltpu.make_async_copy(dr_hbm, dbuf_r, load.at[1]),
    ]
    load_x = pltpu.make_async_copy(spec_hbm, xin, load.at[2])
    load_x.start()
    for item in loads:
        item.start()
    row = pl.ds(0, MESSAGE)
    barrier = pltpu.get_barrier_semaphore()
    plane = [(hop, (r, p)) for hop, p, *_ in others[0]] + [(hop, (across, p)) for hop, p in facing]
    column = [(hop, (p, c)) for hop, p, slot, dy, far in others[1] if not (dy and (far or hop == 1))]
    farthest = lambda devices: [device for _, device in sorted(devices, key=lambda item: -item[0])]
    greeted = farthest(plane + column)
    for device in greeted:
        pl.semaphore_signal(barrier, inc=1, device_id=device, device_id_type=MESH)

    pw_send[...] = jnp.zeros((8, 128), F32)
    load_x.wait()
    tiles = [[[xin[f, p, :, 128 * t : 128 * t + 128].astype(F32) for t in range(2)] for p in range(2)] for f in range(2)]
    lane = lax.broadcasted_iota(jnp.int32, (1, 128), 1)
    column = jnp.zeros((OWN, 128), F32)
    for f in range(2):
        total = sum(tiles[f][p][t] * tiles[f][p][t] for p in range(2) for t in range(2))
        at = lax.broadcasted_iota(jnp.int32, (OWN, 128), 1)
        column = jnp.where(at == f, jnp.sum(total, axis=1, keepdims=True), column)
    rows = jnp.concatenate([column, jnp.zeros((128 - OWN, 128), F32)], axis=0).T
    power = [rows[f : f + 1] for f in range(2)]
    station = (r * SIDE + c) * OWN + lane
    pw_send[:1] = power[0] + pltpu.roll(power[1], OWN, 1)
    for f in range(2):
        mine = (station == wl[f]) & (lane < OWN)
        found = jnp.sum(jnp.where(mine, power[f], 0.0), axis=1, keepdims=True)
        pw_send[1 + f : 2 + f] = jnp.broadcast_to(found, (1, 128))

    pl.semaphore_wait(barrier, len(greeted))

    for device in farthest(plane):
        copy(pw_send.at[row], pw.at[y_lo * SIDE + c, row], PW, device).start()
    pw[y_lo * SIDE + c] = pw_send[...]

    low = lax.broadcasted_iota(jnp.int32, (OWN, 128), 1) < 64
    for f in range(2):
        for t in range(2):
            re, im = tiles[f][0][t], tiles[f][1][t]
            first = jnp.where(low, re, pltpu.roll(im, 64, 1))
            second = jnp.where(low, pltpu.roll(re, 64, 1), im)
            for k, value in ((2 * t, first), (2 * t + 1, second)):
                pk[4 * f + k] = jnp.concatenate([value, jnp.zeros((SLOT - OWN, 128), F32)], axis=0).astype(BF16)
    used = pl.ds(0, OWN)
    for _, p, slot, cross, _ in others[0]:
        if not cross:
            copy(pk.at[slot, used], xr.at[0, core * 8 + c // 2, used], X_ROW, peer(0, p)).start()
    xr[0, core * 8 + c // 2] = pk[slots[0]]
    for _, p, slot, dy, far in sorted(others[1], key=lambda item: not item[4]):
        if not (far and dy):
            copy(pk.at[slot, used], xr.at[1, 8 * dy + z, used], X_FAR if far else X_COL, peer(1, p)).start()
    xr[1, z] = pk[slots[1]]

    def steer(which):
        loads[which].wait()
        rate = jnp.where(slots[which] // 4 == 0, RATES[0], RATES[1]).astype(F32)

        def angles(n):
            q = n % 8 * 2 + n // 8 if which == 0 else (y_lo + n // 8) % 2 * 8 + n % 8
            rows = pl.ds(pl.multiple_of(q * OWN, 8), OWN)
            if which == 0:
                delays = dbuf_s[rows]
            else:
                odd = lax.broadcasted_iota(jnp.int32, (OWN, 128), 1) // 32 % 2
                pairs = [[dbuf_r[rows, 256 * t + 128 * a : 256 * t + 128 * a + 128] for a in range(2)] for t in range(2)]
                delays = jnp.concatenate(
                    [jnp.where(odd == halves[1], a, pltpu.roll(b, 32 + 64 * halves[1], 1)) for a, b in pairs], axis=1
                )
            turns = delays.astype(F32) * rate
            return turns - jnp.round(turns)

        def step(m, carry):
            x = jnp.concatenate([angles(2 * m), angles(2 * m + 1)], axis=0)
            z = x * x
            at = pl.ds(pl.multiple_of(m * 2 * OWN, 2 * OWN), 2 * OWN)
            tab[at, :HALF] = horner(COS, z).astype(BF16)
            tab[at, HALF:] = (horner(SIN, z) * x).astype(BF16)
            return carry

        lax.fori_loop(0, SIDE // 2, step, 0)
        for h in range(2):
            for b in range(SIDE * OWN // 128):
                value = tab[128 * b : 128 * b + 128, HALF * h : HALF * h + HALF].T
                if which == 0:
                    turned_s[HALF * h : HALF * h + HALF, 128 * b : 128 * b + 128] = value
                else:
                    turned_r[:, SIDE * OWN * h + 128 * b : SIDE * OWN * h + 128 * b + 128] = value

    def columns(rows):
        return jnp.concatenate([rows, jnp.zeros((128 - rows.shape[0], 128), F32)], axis=0).T

    steer(0)
    arrived(pw.at[:, row], 2 * SIDE - 1, PW)
    plane_sum = jnp.sum(pw[...], axis=0)
    there = pw[(1 - y_lo) * SIDE + c, :1]
    first = lax.broadcasted_iota(jnp.int32, (8, 128), 0) == 0
    for f in range(2):
        both = jnp.where(lane < OWN, power[f], there if f else pltpu.roll(there, OWN, 1))
        lv_send[f] = jnp.where(first, both, plane_sum)
    for _, p, slot, dy, _ in others[1]:
        if not dy:
            copy(lv_send.at[lax.div(slot, 4), row], lv.at[z, row], LV, peer(1, p)).start()
    lv[z] = lv_send[z // 4]

    arrived(xr.at[1, :, used], 3, X_FAR)
    for d in (4, 3, 5):
        copy(xr.at[1, zs[d], used], xr.at[1, 8 + zs[d], used], X_HAND, (across, c)).start()
    arrived(xr.at[0, :, used], 7, X_ROW)
    half = xr.at[0, pl.ds(core * 8, 8), used]
    copy(half, half, X_CORE, peer(0, c + 1 - 2 * core)).start()
    here = pw[pl.ds(y_lo * SIDE, SIDE), 0, :]
    powers[...] = columns(jnp.where(y_hi == 0, here, pltpu.roll(here, 128 - OWN, 1)))[:OWN]
    steer(1)

    low_x = lax.broadcasted_iota(jnp.int32, (OWN, 128), 1) < 64

    def unpack(axis, start, stop):
        def step(i, carry):
            n = i if axis == 0 else i // 8 * 8 + (z + 6 + i) % 8
            value = xr[axis, n, :OWN].astype(F32)
            xf[axis, pl.ds(pl.multiple_of(n * OWN, 8), OWN)] = value
            if axis == 1:
                value = pltpu.roll(value, 64, 1)
                xf[2, pl.ds(pl.multiple_of(n * OWN, 8), OWN)] = jnp.where(low_x, -value, value)
            return carry

        lax.fori_loop(start, stop, step, 0)

    arrived(xr.at[0, :, used], 8, X_CORE)
    unpack(0, 0, SIDE)
    arrived(xr.at[1, :, used], 9, X_COL)
    unpack(1, 0, SIDE - 3)
    arrived(xr.at[1, :, used], 3, X_HAND)
    unpack(1, SIDE - 3, SIDE)
    arrived(lv.at[:, row], 7, LV)
    marks = 0.5 * jnp.sum(lv[...], axis=0)
    level = [jnp.where(slots[which] // 4 == 0, marks[1:2], marks[2:3]) for which in range(2)]

    gain = lax.rsqrt(powers[...] + level[0])
    scaled = [
        xf[0, OWN * n : OWN * n + OWN] * gain[:, n % 8 * 2 + n // 8 : n % 8 * 2 + n // 8 + 1] for n in range(SIDE)
    ]
    both = jnp.dot(turned_s[...], jnp.concatenate(scaled, axis=0).astype(BF16), preferred_element_type=F32)
    low = lax.broadcasted_iota(jnp.int32, (HALF, 128), 1) < 64
    swapped = pltpu.roll(both[HALF:], 64, 1)
    value = (both[:HALF] + jnp.where(low, -swapped, swapped)).astype(BF16)
    for j in range(8):
        sums_s[j] = value[BEAMS * j : BEAMS * j + BEAMS]
    for d in RINGS[0][:-1]:
        copy(sums_s.at[zs[d]], part.at[0, r], SUM_U, peer(1, (1 - core) * 8 + zs[d])).start()

    gain = lax.rsqrt(columns(lv[:, 0, :])[: 2 * OWN] + level[1])
    scaled = []
    for side in (1, 2):
        for n in range(SIDE):
            own = gain[n // 8 * OWN : n // 8 * OWN + OWN, n % 8 : n % 8 + 1]
            scaled.append(xf[side, OWN * n : OWN * n + OWN] * own)
    value = jnp.dot(
        turned_r[...], jnp.concatenate(scaled, axis=0).astype(BF16), preferred_element_type=F32
    ).astype(BF16)
    for j in range(8):
        sums_r[j] = value[BEAMS * j : BEAMS * j + BEAMS]
    for dx, dy in ((dx, dy) for dx in RINGS[1] for dy in (1, 0)):
        y, xx, h = flip(y_hi, dy), lax.div(xs[dx], 2), halves[1]
        a = lax.div(xx, 2)
        j = 4 * y + 2 * lax.rem(xx, 2) + a + h - 2 * a * h
        copy(sums_r.at[j], part.at[1, c], SUM_V, (across, y * 8 + xs[dx] + h)).start()

    @pl.when(jnp.logical_not(holder[0]))
    def _():
        copy(sums_s.at[z], part.at[0, r], SUM_U, peer(1, across)).start()

    @pl.when(holder[0])
    def _():
        part[0, r] = sums_s[z]

    def total(which):
        value = jnp.sum(part[which].astype(F32), axis=0).astype(BF16)
        block[which] = value
        return value

    @pl.when(holder[1])
    def _():
        arrived(part.at[1], SIDE, SUM_V)
        value = total(1)
        for _, p, *_ in others[1]:
            copy(block.at[1], gathered.at[1, z], ALL_V, peer(1, p)).start()
        gathered[1, z] = value

    @pl.when(holder[0])
    def _():
        arrived(part.at[0], SIDE - 1, SUM_U)
        total(0)
        for _, p in facing:
            copy(block.at[0], gathered.at[0, slots[0]], ALL_U, (across, p)).start()

    arrived(gathered.at[0], 8, ALL_U)
    low = lax.broadcasted_iota(jnp.int32, (BEAMS, 128), 1) < 64
    for k in range(8):
        u = gathered[0, k].astype(F32)
        swapped = pltpu.roll(u, 64, 1)
        swapped = jnp.where(low, swapped, -swapped)
        right[k // 4, 128 * (k % 4) : 128 * (k % 4) + 128] = jnp.concatenate(
            [u, swapped, jnp.zeros((64, 128), F32)], axis=0
        ).T.astype(BF16)
    left(pw.at[:, row], 2 * SIDE - 1, PW)
    left(xr.at[0, :, used], 7, X_ROW)
    left(xr.at[0, :, used], 8, X_CORE)
    left(xr.at[1, :, used], 9, X_COL)
    left(xr.at[1, :, used], 3, X_FAR)
    left(xr.at[1, :, used], 3, X_HAND)
    left(lv.at[:, row], 7, LV)
    left(part.at[1], 8, SUM_V)

    @pl.when(holder[0])
    def _():
        left(part.at[0], 7, SUM_U)
        left(part.at[0], SIDE, ALL_U)
        arrived(gathered.at[1], 8, ALL_V)

    @pl.when(holder[1])
    def _():
        left(part.at[0], 8, SUM_U)
        left(part.at[1], SIDE - 1, ALL_V)
        arrived(gathered.at[1], 7, ALL_V)

    for f in range(2):
        v = jnp.concatenate([gathered[1, 4 * f + k] for k in range(4)], axis=1)
        value = jnp.dot(v, right[f, :, : 2 * BEAMS], preferred_element_type=F32) * (math.sqrt(WINDOWS) / STATIONS)
        out[f, 0] = value[:, :BEAMS]
        out[f, 1] = value[:, BEAMS:]


def body(spectra, delays_s, delays_r, wl_index):
    return pl.pallas_call(
        kernel,
        out_shape=pltpu.VMEM((2, 2, BEAMS, BEAMS), F32),
        in_specs=[pl.BlockSpec(memory_space=pl.ANY)] * 3 + [pl.BlockSpec(memory_space=pltpu.SMEM)],
        out_specs=pl.BlockSpec(memory_space=pltpu.VMEM),
        scratch_shapes=[
            pltpu.VMEM((2, 2, OWN, WINDOWS), BF16),
            pltpu.VMEM((SIDE * OWN, HALF), jnp.int32),
            pltpu.VMEM((SIDE * OWN, 2 * HALF), jnp.int32),
            pltpu.VMEM((SIDE * OWN, 2 * HALF), BF16),
            pltpu.VMEM((2 * HALF, SIDE * OWN), BF16),
            pltpu.VMEM((HALF, 2 * SIDE * OWN), BF16),
            pltpu.VMEM((8, SLOT, 128), BF16),
            pltpu.VMEM((2, SIDE, SLOT, 128), BF16),
            pltpu.VMEM((3, SIDE * OWN, 128), F32),
            pltpu.VMEM((8, 128), F32),
            pltpu.VMEM((2 * SIDE, 8, 128), F32),
            pltpu.VMEM((OWN, 128), F32),
            pltpu.VMEM((2, 8, 128), F32),
            pltpu.VMEM((8, 8, 128), F32),
            pltpu.VMEM((8, BEAMS, 128), BF16),
            pltpu.VMEM((8, BEAMS, 128), BF16),
            pltpu.VMEM((2, SIDE, BEAMS, 128), BF16),
            pltpu.VMEM((2, BEAMS, 128), BF16),
            pltpu.VMEM((2, 8, BEAMS, 128), BF16),
            pltpu.VMEM((2, 512, 128), BF16),
            pltpu.SemaphoreType.DMA((3,)),
            pltpu.SemaphoreType.DMA((11,)),
            pltpu.SemaphoreType.DMA((11,)),
        ],
        compiler_params=pltpu.CompilerParams(collective_id=0, has_side_effects=True),
    )(spectra, delays_s, delays_r, wl_index)


def solution(mesh):
    in_specs = (P(None, None, ("row", "col"), None), P("row", None), P("col", None), P())
    out_specs = P(None, None, "col", "row")
    return jax.shard_map(body, mesh=mesh, in_specs=in_specs, out_specs=out_specs, check_vma=False)
```

```python
import functools
import math

import jax
import jax.numpy as jnp
from jax import lax
from jax.experimental import pallas as pl
from jax.experimental.pallas import tpu as pltpu
from jax.sharding import PartitionSpec as P

MESH = pl.DeviceIdType.MESH
F32 = jnp.float32
BF16 = jnp.bfloat16

STATIONS = 10240
WINDOWS = 256
SIDE = 16
OWN = 40
SLOT = 48
HALF = 256
BEAMS = 32
RATES = (0.0361, 0.0596)

COS = (0.9999992215668542, -19.7389825153523, 64.92872658489378, -85.27239662504564, 58.79403695210448, -21.076779298561963)
SIN = (6.283182818541802, -41.34142139793358, 81.59618385577838, -76.58010036540968, 41.20539421297601, -12.271261390344423)

PW, X_ROW, X_CORE, X_COL, X_FAR, X_HAND, LV, SUM_U, SUM_V, ALL_U, ALL_V = range(11)
RINGS = ((4, 3, 5, 2, 6, 1, 7, 0), (2, 1, 3, 0))
MESSAGE = 3


def horner(coefs, z):
    acc = jnp.full_like(z, coefs[-1])
    for c in coefs[-2::-1]:
        acc = acc * z + c
    return acc


def kernel(
    spec_hbm, ds_hbm, dr_hbm, wl, out,
    xin, dbuf_s, dbuf_r, tab, turned_s, turned_r, pk, xr, xf, pw_send, pw, powers, lv_send, lv, sums_s, sums_r, part, block, gathered, right,
    load, send, recv,
):
    r, c = lax.axis_index("row"), lax.axis_index("col")
    (y_lo, z), (y_hi, x, core) = (r // 8, r % 8), (c // 8, c // 2 % 4, c % 2)
    slots = (c // 2, z)
    halves = (core, 1 - y_lo)
    holder = (core != y_lo, core == y_lo)
    across = (1 - y_lo) * 8 + z

    def peer(axis, other):
        return (r, other) if axis == 0 else (other, c)

    zs = {d: lax.rem(z + d, 8) for d in RINGS[0]}
    xs = {d: lax.rem(x + d, 4) * 2 for d in RINGS[1]}
    flip = lambda bit, d: 1 - bit if d else bit
    hops = lambda d, n: min(d, n - d)
    others, facing = ([], []), []
    for dx, dy, dc in sorted(
        ((dx, dy, dc) for dx in RINGS[1] for dy in (1, 0) for dc in (1, 0)), key=lambda d: -hops(d[0], 4) - 2 * d[1]
    ):
        y = flip(y_hi, dy)
        p = y * 8 + xs[dx] + flip(core, dc)
        if dx or dy or dc:
            others[0].append((hops(dx, 4) + 2 * dy, p, y * 4 + lax.div(xs[dx], 2), dc, False))
        facing.append((hops(dx, 4) + 1, p))
    facing.sort(key=lambda item: -item[0])
    for dz, dy in sorted(((dz, dy) for dz in RINGS[0] for dy in (1, 0)), key=lambda d: -hops(d[0], 8) - d[1]):
        if dz or dy:
            others[1].append((hops(dz, 8) + dy, flip(y_lo, dy) * 8 + zs[dz], zs[dz], dy, hops(dz, 8) > 2))

    def copy(src, dst, group, device):
        return pltpu.make_async_remote_copy(
            src_ref=src, dst_ref=dst, send_sem=send.at[group], recv_sem=recv.at[group],
            device_id=device, device_id_type=MESH,
        )

    def arrived(ref, n, group):
        copy(ref.at[pl.ds(0, n)], ref.at[pl.ds(0, n)], group, (r, c)).wait_recv()

    def left(ref, n, group):
        copy(ref.at[pl.ds(0, n)], ref.at[pl.ds(0, n)], group, (r, c)).wait_send()

    start = pl.multiple_of(halves[0] * HALF, HALF)
    loads = [
        pltpu.make_async_copy(ds_hbm.at[:, pl.ds(start, HALF)], dbuf_s, load.at[0]),
        pltpu.make_async_copy(dr_hbm, dbuf_r, load.at[1]),
    ]
    load_x = pltpu.make_async_copy(spec_hbm, xin, load.at[2])
    load_x.start()
    row = pl.ds(0, MESSAGE)
    barrier = pltpu.get_barrier_semaphore()
    plane = [(hop, (r, p)) for hop, p, *_ in others[0]] + [(hop, (across, p)) for hop, p in facing]
    column = [(hop, (p, c)) for hop, p, slot, dy, far in others[1] if not (dy and (far or hop == 1))]
    farthest = lambda devices: [device for _, device in sorted(devices, key=lambda item: -item[0])]
    greeted = farthest(column + plane)
    for device in greeted:
        pl.semaphore_signal(barrier, inc=1, device_id=device, device_id_type=MESH)
    for item in loads:
        item.start()

    pw_send[...] = jnp.zeros((8, 128), F32)
    load_x.wait()
    tiles = [[[xin[f, p, :, 128 * t : 128 * t + 128].astype(F32) for t in range(2)] for p in range(2)] for f in range(2)]
    lane = lax.broadcasted_iota(jnp.int32, (1, 128), 1)
    column = jnp.zeros((OWN, 128), F32)
    for f in range(2):
        total = sum(tiles[f][p][t] * tiles[f][p][t] for p in range(2) for t in range(2))
        at = lax.broadcasted_iota(jnp.int32, (OWN, 128), 1)
        column = jnp.where(at == f, jnp.sum(total, axis=1, keepdims=True), column)
    rows = jnp.concatenate([column, jnp.zeros((128 - OWN, 128), F32)], axis=0).T
    power = [rows[f : f + 1] for f in range(2)]
    station = (r * SIDE + c) * OWN + lane
    pw_send[:1] = power[0] + pltpu.roll(power[1], OWN, 1)
    for f in range(2):
        mine = (station == wl[f]) & (lane < OWN)
        found = jnp.sum(jnp.where(mine, power[f], 0.0), axis=1, keepdims=True)
        pw_send[1 + f : 2 + f] = jnp.broadcast_to(found, (1, 128))

    pl.semaphore_wait(barrier, len(greeted))

    for device in farthest(plane):
        copy(pw_send.at[row], pw.at[y_lo * SIDE + c, row], PW, device).start()
    pw[y_lo * SIDE + c] = pw_send[...]

    low = lax.broadcasted_iota(jnp.int32, (OWN, 128), 1) < 64
    for f in range(2):
        for t in range(2):
            re, im = tiles[f][0][t], tiles[f][1][t]
            first = jnp.where(low, re, pltpu.roll(im, 64, 1))
            second = jnp.where(low, pltpu.roll(re, 64, 1), im)
            for k, value in ((2 * t, first), (2 * t + 1, second)):
                pk[4 * f + k] = jnp.concatenate([value, jnp.zeros((SLOT - OWN, 128), F32)], axis=0).astype(BF16)
    used = pl.ds(0, OWN)
    for _, p, slot, cross, _ in others[0]:
        if not cross:
            copy(pk.at[slot, used], xr.at[0, core * 8 + c // 2, used], X_ROW, peer(0, p)).start()
    xr[0, core * 8 + c // 2] = pk[slots[0]]
    for _, p, slot, dy, far in sorted(others[1], key=lambda item: not item[4]):
        if not (far and dy):
            copy(pk.at[slot, used], xr.at[1, 8 * dy + z, used], X_FAR if far else X_COL, peer(1, p)).start()
    xr[1, z] = pk[slots[1]]

    def steer(which):
        loads[which].wait()
        rate = jnp.where(slots[which] // 4 == 0, RATES[0], RATES[1]).astype(F32)

        def angles(n):
            q = n % 8 * 2 + n // 8 if which == 0 else (y_lo + n // 8) % 2 * 8 + n % 8
            rows = pl.ds(pl.multiple_of(q * OWN, 8), OWN)
            if which == 0:
                delays = dbuf_s[rows]
            else:
                odd = lax.broadcasted_iota(jnp.int32, (OWN, 128), 1) // 32 % 2
                pairs = [[dbuf_r[rows, 256 * t + 128 * a : 256 * t + 128 * a + 128] for a in range(2)] for t in range(2)]
                delays = jnp.concatenate(
                    [jnp.where(odd == halves[1], a, pltpu.roll(b, 32 + 64 * halves[1], 1)) for a, b in pairs], axis=1
                )
            turns = delays.astype(F32) * rate
            return turns - jnp.round(turns)

        def step(m, carry):
            x = jnp.concatenate([angles(2 * m), angles(2 * m + 1)], axis=0)
            z = x * x
            at = pl.ds(pl.multiple_of(m * 2 * OWN, 2 * OWN), 2 * OWN)
            tab[at, :HALF] = horner(COS, z).astype(BF16)
            tab[at, HALF:] = (horner(SIN, z) * x).astype(BF16)
            return carry

        lax.fori_loop(0, SIDE // 2, step, 0)
        for h in range(2):
            for b in range(SIDE * OWN // 128):
                value = tab[128 * b : 128 * b + 128, HALF * h : HALF * h + HALF].T
                if which == 0:
                    turned_s[HALF * h : HALF * h + HALF, 128 * b : 128 * b + 128] = value
                else:
                    turned_r[:, SIDE * OWN * h + 128 * b : SIDE * OWN * h + 128 * b + 128] = value

    def columns(rows):
        return jnp.concatenate([rows, jnp.zeros((128 - rows.shape[0], 128), F32)], axis=0).T

    steer(0)
    arrived(pw.at[:, row], 2 * SIDE - 1, PW)
    plane_sum = jnp.sum(pw[...], axis=0)
    there = pw[(1 - y_lo) * SIDE + c, :1]
    first = lax.broadcasted_iota(jnp.int32, (8, 128), 0) == 0
    for f in range(2):
        both = jnp.where(lane < OWN, power[f], there if f else pltpu.roll(there, OWN, 1))
        lv_send[f] = jnp.where(first, both, plane_sum)
    for _, p, slot, dy, _ in others[1]:
        if not dy:
            copy(lv_send.at[lax.div(slot, 4), row], lv.at[z, row], LV, peer(1, p)).start()
    lv[z] = lv_send[z // 4]

    arrived(xr.at[1, :, used], 3, X_FAR)
    for d in (4, 3, 5):
        copy(xr.at[1, zs[d], used], xr.at[1, 8 + zs[d], used], X_HAND, (across, c)).start()
    arrived(xr.at[0, :, used], 7, X_ROW)
    half = xr.at[0, pl.ds(core * 8, 8), used]
    copy(half, half, X_CORE, peer(0, c + 1 - 2 * core)).start()
    here = pw[pl.ds(y_lo * SIDE, SIDE), 0, :]
    powers[...] = columns(jnp.where(y_hi == 0, here, pltpu.roll(here, 128 - OWN, 1)))[:OWN]
    steer(1)

    low_x = lax.broadcasted_iota(jnp.int32, (OWN, 128), 1) < 64

    def unpack(axis, start, stop):
        def step(i, carry):
            n = i if axis == 0 else i // 8 * 8 + (z + 6 + i) % 8
            value = xr[axis, n, :OWN].astype(F32)
            xf[axis, pl.ds(pl.multiple_of(n * OWN, 8), OWN)] = value
            if axis == 1:
                value = pltpu.roll(value, 64, 1)
                xf[2, pl.ds(pl.multiple_of(n * OWN, 8), OWN)] = jnp.where(low_x, -value, value)
            return carry

        lax.fori_loop(start, stop, step, 0)

    arrived(xr.at[0, :, used], 8, X_CORE)
    unpack(0, 0, SIDE)
    arrived(xr.at[1, :, used], 9, X_COL)
    unpack(1, 0, SIDE - 3)
    arrived(xr.at[1, :, used], 3, X_HAND)
    unpack(1, SIDE - 3, SIDE)
    arrived(lv.at[:, row], 7, LV)
    marks = 0.5 * jnp.sum(lv[...], axis=0)
    level = [jnp.where(slots[which] // 4 == 0, marks[1:2], marks[2:3]) for which in range(2)]

    gain = lax.rsqrt(powers[...] + level[0])
    scaled = [
        xf[0, OWN * n : OWN * n + OWN] * gain[:, n % 8 * 2 + n // 8 : n % 8 * 2 + n // 8 + 1] for n in range(SIDE)
    ]
    both = jnp.dot(turned_s[...], jnp.concatenate(scaled, axis=0).astype(BF16), preferred_element_type=F32)
    low = lax.broadcasted_iota(jnp.int32, (HALF, 128), 1) < 64
    swapped = pltpu.roll(both[HALF:], 64, 1)
    value = (both[:HALF] + jnp.where(low, -swapped, swapped)).astype(BF16)
    for j in range(8):
        sums_s[j] = value[BEAMS * j : BEAMS * j + BEAMS]
    for d in RINGS[0][:-1]:
        copy(sums_s.at[zs[d]], part.at[0, r], SUM_U, peer(1, (1 - core) * 8 + zs[d])).start()

    gain = lax.rsqrt(columns(lv[:, 0, :])[: 2 * OWN] + level[1])
    scaled = []
    for side in (1, 2):
        for n in range(SIDE):
            own = gain[n // 8 * OWN : n // 8 * OWN + OWN, n % 8 : n % 8 + 1]
            scaled.append(xf[side, OWN * n : OWN * n + OWN] * own)
    value = jnp.dot(
        turned_r[...], jnp.concatenate(scaled, axis=0).astype(BF16), preferred_element_type=F32
    ).astype(BF16)
    for j in range(8):
        sums_r[j] = value[BEAMS * j : BEAMS * j + BEAMS]
    for dx, dy in ((dx, dy) for dx in RINGS[1] for dy in (1, 0)):
        y, xx, h = flip(y_hi, dy), lax.div(xs[dx], 2), halves[1]
        a = lax.div(xx, 2)
        j = 4 * y + 2 * lax.rem(xx, 2) + a + h - 2 * a * h
        copy(sums_r.at[j], part.at[1, c], SUM_V, (across, y * 8 + xs[dx] + h)).start()

    @pl.when(jnp.logical_not(holder[0]))
    def _():
        copy(sums_s.at[z], part.at[0, r], SUM_U, peer(1, across)).start()

    @pl.when(holder[0])
    def _():
        part[0, r] = sums_s[z]

    def total(which):
        value = jnp.sum(part[which].astype(F32), axis=0).astype(BF16)
        block[which] = value
        return value

    @pl.when(holder[1])
    def _():
        arrived(part.at[1], SIDE, SUM_V)
        value = total(1)
        for _, p, *_ in others[1]:
            copy(block.at[1], gathered.at[1, z], ALL_V, peer(1, p)).start()
        gathered[1, z] = value

    @pl.when(holder[0])
    def _():
        arrived(part.at[0], SIDE - 1, SUM_U)
        total(0)
        for _, p in facing:
            copy(block.at[0], gathered.at[0, slots[0]], ALL_U, (across, p)).start()

    arrived(gathered.at[0], 8, ALL_U)
    low = lax.broadcasted_iota(jnp.int32, (BEAMS, 128), 1) < 64
    for k in range(8):
        u = gathered[0, k].astype(F32)
        swapped = pltpu.roll(u, 64, 1)
        swapped = jnp.where(low, swapped, -swapped)
        right[k // 4, 128 * (k % 4) : 128 * (k % 4) + 128] = jnp.concatenate(
            [u, swapped, jnp.zeros((64, 128), F32)], axis=0
        ).T.astype(BF16)
    left(pw.at[:, row], 2 * SIDE - 1, PW)
    left(xr.at[0, :, used], 7, X_ROW)
    left(xr.at[0, :, used], 8, X_CORE)
    left(xr.at[1, :, used], 9, X_COL)
    left(xr.at[1, :, used], 3, X_FAR)
    left(xr.at[1, :, used], 3, X_HAND)
    left(lv.at[:, row], 7, LV)
    left(part.at[1], 8, SUM_V)

    @pl.when(holder[0])
    def _():
        left(part.at[0], 7, SUM_U)
        left(part.at[0], SIDE, ALL_U)
        arrived(gathered.at[1], 8, ALL_V)

    @pl.when(holder[1])
    def _():
        left(part.at[0], 8, SUM_U)
        left(part.at[1], SIDE - 1, ALL_V)
        arrived(gathered.at[1], 7, ALL_V)

    for f in range(2):
        v = jnp.concatenate([gathered[1, 4 * f + k] for k in range(4)], axis=1)
        value = jnp.dot(v, right[f, :, : 2 * BEAMS], preferred_element_type=F32) * (math.sqrt(WINDOWS) / STATIONS)
        out[f, 0] = value[:, :BEAMS]
        out[f, 1] = value[:, BEAMS:]


def body(spectra, delays_s, delays_r, wl_index):
    return pl.pallas_call(
        kernel,
        out_shape=pltpu.VMEM((2, 2, BEAMS, BEAMS), F32),
        in_specs=[pl.BlockSpec(memory_space=pl.ANY)] * 3 + [pl.BlockSpec(memory_space=pltpu.SMEM)],
        out_specs=pl.BlockSpec(memory_space=pltpu.VMEM),
        scratch_shapes=[
            pltpu.VMEM((2, 2, OWN, WINDOWS), BF16),
            pltpu.VMEM((SIDE * OWN, HALF), jnp.int32),
            pltpu.VMEM((SIDE * OWN, 2 * HALF), jnp.int32),
            pltpu.VMEM((SIDE * OWN, 2 * HALF), BF16),
            pltpu.VMEM((2 * HALF, SIDE * OWN), BF16),
            pltpu.VMEM((HALF, 2 * SIDE * OWN), BF16),
            pltpu.VMEM((8, SLOT, 128), BF16),
            pltpu.VMEM((2, SIDE, SLOT, 128), BF16),
            pltpu.VMEM((3, SIDE * OWN, 128), F32),
            pltpu.VMEM((8, 128), F32),
            pltpu.VMEM((2 * SIDE, 8, 128), F32),
            pltpu.VMEM((OWN, 128), F32),
            pltpu.VMEM((2, 8, 128), F32),
            pltpu.VMEM((8, 8, 128), F32),
            pltpu.VMEM((8, BEAMS, 128), BF16),
            pltpu.VMEM((8, BEAMS, 128), BF16),
            pltpu.VMEM((2, SIDE, BEAMS, 128), BF16),
            pltpu.VMEM((2, BEAMS, 128), BF16),
            pltpu.VMEM((2, 8, BEAMS, 128), BF16),
            pltpu.VMEM((2, 512, 128), BF16),
            pltpu.SemaphoreType.DMA((3,)),
            pltpu.SemaphoreType.DMA((11,)),
            pltpu.SemaphoreType.DMA((11,)),
        ],
        compiler_params=pltpu.CompilerParams(collective_id=0, has_side_effects=True),
    )(spectra, delays_s, delays_r, wl_index)


def solution(mesh):
    in_specs = (P(None, None, ("row", "col"), None), P("row", None), P("col", None), P())
    out_specs = P(None, None, "col", "row")
    return jax.shard_map(body, mesh=mesh, in_specs=in_specs, out_specs=out_specs, check_vma=False)
```
